128 devices in a mesh: grp: 8 (over z, core), col: 16 (over x, y).
Axes of the slice: x: 4, y: 4, z: 4, core: 2. Of those that a mesh axis runs over, the one named last changes fastest.
Arguments:
- pivot_blocks: float32 [8, 1024, 1024], P('grp'), as said below
- coupling: float32 [8, 4096, 1024], P('grp', 'col'), as said below
- block_map: int32 [8, 32], replicated, may hold values from 0 to 63, as said below
- parent_matrix: float32 [8192, 8192], P('grp', 'col'), as said below
Outputs:
- child_factor: float32 [8, 4096, 1024], P('grp', 'col')
- parent_factor: float32 [8192, 8192], P('grp', 'col')
The draws below stay inside these ranges and needn't reach their ends.
Inputs may be any that keep to these rules, and one draw needn't show every extreme that they name: `block_map`: each row is strictly increasing. For every child and every aligned run of 8 parent blocks (starting at a multiple of 8), at most 6 of the row's entries fall in the run; one such run holds exactly 6 entries of every row. `pivot_blocks`: every child's block is symmetric positive definite. `coupling`: independent entries. `parent_matrix`: Symmetric, with a positive diagonal; the leading 2 * 512 rows and columns of assembled form a positive definite block.
All inputs are finite; a program needn't handle non-finite values.
Results may differ from the reference program's by a relative error of at most 0.0001.
Values sent between devices are 32-bit elements; how exact they have to be, the bound alone decides.
No kernel may reach another device: no remote copies, remote signals or barrier semaphores. Data moves between devices by JAX's collectives and lax.ppermute only.
A program may use at most 128 MiB of HBM per device.

```python
import math
import jax
import jax.numpy as jnp
from jax import lax

BLK = 128
PIV = 1024
SCH = 4096
PAR = 8192
PANEL = 512
PANELS = 2
CHILDREN = 8
SBLK = 32
RBK = 8
MOSTR = 6
N_GRP = 8


def unit_symmetric(key, order):
    random_part = jax.random.normal(key, (order, order), jnp.float32)
    mirrored = (random_part + random_part.T) * (1.0 / math.sqrt(2.0))
    return mirrored * (1.0 - jnp.eye(order, dtype=jnp.float32))


def wishart_part(key, order):
    factor = jax.random.normal(key, (order, 2 * order), jnp.float32)
    product = jnp.dot(factor, factor.T, precision=lax.Precision.HIGHEST, preferred_element_type=jnp.float32) * (1.0 / (2.0 * order))
    return (product + product.T) * 0.5


def draw_pivot_blocks(key, part):
    child_keys = jax.random.split(jax.random.fold_in(key, 3), CHILDREN)

    def one_child(child_key):
        key_diag, key_off = jax.random.split(child_key)
        diagonal = jax.random.uniform(key_diag, (PIV,), jnp.float32, 0.15, 0.3)
        return wishart_part(key_off, PIV) + jnp.diag(diagonal)
    return jax.vmap(one_child)(child_keys)


def draw_coupling(key, part):
    spread = math.sqrt(0.16 / PIV)
    inner_key = jax.random.fold_in(key, 5)
    values = jnp.clip(jax.random.normal(inner_key, (CHILDREN, SCH, PIV), jnp.float32), -5.0, 5.0)
    return values * spread


def draw_parent_matrix(key, part):
    key_diag, key_off, key_lead, key_lead_diag = jax.random.split(jax.random.fold_in(key, 11), 4)
    leading = PANELS * PANEL
    inside = jnp.arange(PAR) < leading
    crossing = inside[:, None] != inside[None, :]
    entry_spread = jnp.where(crossing, 8.0, 0.8) * (1.0 / math.sqrt(leading))
    diagonal = jax.random.uniform(key_diag, (PAR,), jnp.float32, 7.0, 10.0)
    base = unit_symmetric(key_off, PAR) * entry_spread + jnp.diag(diagonal)
    lead_diagonal = jax.random.uniform(key_lead_diag, (leading,), jnp.float32, 9.0, 11.0)
    lead_block = 30.0 * wishart_part(key_lead, leading) + jnp.diag(lead_diagonal)
    return base.at[:leading, :leading].set(lead_block)


def draw_block_map(key, part):
    busy_owner = jax.random.randint(jax.random.fold_in(key, 7), (), 0, N_GRP)

    def one_child(child_key):
        key_bias, key_shuffle, key_rank = jax.random.split(child_key, 3)
        owner_bias = jax.random.randint(key_bias, (N_GRP,), 0, 4)
        shuffle = jax.random.permutation(key_shuffle, N_GRP * MOSTR)
        scores = (jnp.repeat(owner_bias, MOSTR) * (N_GRP * MOSTR) + shuffle).reshape(N_GRP, MOSTR)
        scores = jnp.where(jnp.arange(N_GRP)[:, None] == busy_owner, -1, scores)
        flattened = scores.reshape(-1).astype(jnp.int32)
        unused_values, winners = lax.top_k(flattened, SBLK - MOSTR)
        selected = jnp.zeros((N_GRP * MOSTR,), jnp.int32).at[winners].set(1).reshape(N_GRP, MOSTR)
        per_owner = jnp.sum(selected, axis=1)
        per_owner = jnp.where(jnp.arange(N_GRP) == busy_owner, MOSTR, per_owner)
        rank_table = jax.vmap(lambda rank_key: jax.random.permutation(rank_key, RBK))(jax.random.split(key_rank, N_GRP))
        chosen_mask = (rank_table < per_owner[:, None]).reshape(-1)
        return jnp.nonzero(chosen_mask, size=SBLK)[0].astype(jnp.int32)
    return jax.vmap(one_child)(jax.random.split(key, CHILDREN))


def setup_inputs(seed: int = 0) -> dict:
    key_list = jax.random.split(jax.random.key(seed), 5)
    pivot_blocks = draw_pivot_blocks(jax.random.fold_in(key_list[4], 71), 0)
    coupling = draw_coupling(jax.random.fold_in(key_list[4], 71), 0)
    block_map = draw_block_map(jax.random.fold_in(key_list[4], 71), 0)
    parent_matrix = draw_parent_matrix(jax.random.fold_in(key_list[4], 71), 0)
    return dict(pivot_blocks=pivot_blocks, coupling=coupling, block_map=block_map, parent_matrix=parent_matrix)


HIGH = lax.Precision.HIGHEST

def reference(pivot_blocks, coupling, block_map, parent_matrix):
    factors = []
    assembled = parent_matrix.reshape(PAR // BLK, BLK, PAR // BLK, BLK)
    for child_index in range(CHILDREN):
        lower_factor = jnp.linalg.cholesky(pivot_blocks[child_index])
        child_rows = lax.linalg.triangular_solve(lower_factor, coupling[child_index], left_side=False, lower=True, transpose_a=True)
        factors.append(child_rows)
        schur_block = -jnp.dot(child_rows.astype(jnp.float32), child_rows.T.astype(jnp.float32), precision=HIGH, preferred_element_type=jnp.float32)
        blocks = schur_block.reshape(SCH // BLK, BLK, SCH // BLK, BLK).transpose(0, 2, 1, 3)
        mapping = block_map[child_index]
        assembled = assembled.at[mapping[:, None], :, mapping[None, :], :].add(blocks)
    matrix = assembled.reshape(PAR, PAR)
    for panel_index in range(PANELS):
        opening = panel_index * PANEL
        closing = opening + PANEL
        lower_factor = jnp.linalg.cholesky(matrix[opening:closing, opening:closing])
        below_rows = lax.linalg.triangular_solve(lower_factor, matrix[closing:, opening:closing], left_side=False, lower=True, transpose_a=True)
        matrix = matrix.at[closing:, closing:].add(-jnp.dot(below_rows.astype(jnp.float32), below_rows.T.astype(jnp.float32), precision=HIGH, preferred_element_type=jnp.float32))
        matrix = matrix.at[opening:closing, opening:closing].set(lower_factor)
        matrix = matrix.at[closing:, opening:closing].set(below_rows)
    return (jnp.stack(factors), matrix)
```

```python
import functools

import jax
import jax.numpy as jnp
from jax import lax
from jax.experimental import pallas as pl
from jax.experimental.pallas import tpu as pltpu
from jax.sharding import PartitionSpec as P

BLK = 128
PANEL = 512
LEAD = 1024
PIV = 1024
SBLK = 32
PBLK = 64
RBK = 8
MOSTR = 6

HIGHEST = lax.Precision.HIGHEST
HIGH = lax.Precision.HIGH


def eliminate(work):
    order = BLK
    lane = lax.broadcasted_iota(jnp.int32, (8, order), 1)
    sub = lax.broadcasted_iota(jnp.int32, (8, order), 0)
    parts = order // 8
    rows = [work[8 * q : 8 * q + 8, :] for q in range(parts)]
    low = [jnp.zeros((8, order), jnp.float32) for q in range(parts)]
    for q in range(parts):
        cols = [
            [
                jnp.broadcast_to(rows[p][:, 8 * q + k : 8 * q + k + 1], (8, order))
                for p in range(q, parts)
            ]
            for k in range(8)
        ]
        here = (lane >= 8 * q) & (lane < 8 * q + 8)
        mine = jnp.where(here, jnp.where(lane == sub + 8 * q, 1.0, 0.0), rows[q])
        fresh = []
        for k in range(8):
            root = lax.rsqrt(jnp.broadcast_to(cols[k][0][k : k + 1, :], (8, order)))
            cols[k] = [c * root for c in cols[k]]
            cols[k][0] = jnp.where(sub >= k, cols[k][0], 0.0)
            for m in range(k + 1, 8):
                scale = jnp.broadcast_to(cols[k][0][m : m + 1, :], (8, order))
                cols[m] = [a - b * scale for a, b in zip(cols[m], cols[k])]
            scaled = mine * root
            row = jnp.broadcast_to(scaled[k : k + 1, :], (8, order))
            fresh.append(row)
            mine = jnp.where(sub > k, mine - cols[k][0] * row, jnp.where(sub == k, scaled, mine))
        rows[q] = mine
        for p in range(q, parts):
            for k in range(8):
                low[p] = jnp.where(lane == 8 * q + k, cols[k][p - q], low[p])
        for p in range(q + 1, parts):
            acc = jnp.where(here, 0.0, rows[p])
            for k in range(8):
                acc = acc - cols[k][p - q] * fresh[k]
            rows[p] = acc
    for q in range(parts):
        rows[q] = jnp.where(lane <= sub + 8 * q, rows[q], 0.0)
    return jnp.concatenate(rows, axis=0), jnp.concatenate(low, axis=0)


def exact(a, b):
    return jnp.dot(a, b, precision=HIGHEST, preferred_element_type=jnp.float32)


def factor_kernel(blocks, want_low, a_ref, *refs):
    if want_low:
        t_ref, l_ref, r_ref = refs
    else:
        t_ref, r_ref = refs
    order = blocks * BLK
    t_ref[...] = a_ref[...]

    def step(b, carry):
        at = pl.multiple_of(b * BLK, BLK)
        inv, low = eliminate(t_ref[pl.ds(at, BLK), pl.ds(at, BLK)])
        r_ref[...] = exact(inv, t_ref[pl.ds(at, BLK), :])
        r_ref[:, pl.ds(at, BLK)] = inv
        t_ref[pl.ds(at, BLK), :] = r_ref[...]
        if want_low:
            l_ref[:, pl.ds(at, BLK)] = jnp.zeros((order, BLK), jnp.float32)
            l_ref[pl.ds(at, BLK), pl.ds(at, BLK)] = low

        def below(i, carry):
            to = pl.multiple_of(i * BLK, BLK)
            left = r_ref[:, pl.ds(to, BLK)].T
            if want_low:
                l_ref[pl.ds(to, BLK), pl.ds(at, BLK)] = left
            t_ref[pl.ds(to, BLK), pl.ds(at, BLK)] = jnp.zeros((BLK, BLK), jnp.float32)
            t_ref[pl.ds(to, BLK), :] = t_ref[pl.ds(to, BLK), :] - exact(left, r_ref[...])
            return carry

        return lax.fori_loop(b + 1, blocks, below, carry)

    lax.fori_loop(0, blocks, step, 0)
    for b in range(blocks - 1):
        width = order - BLK * (b + 1)
        t_ref[BLK * b : BLK * b + BLK, BLK * (b + 1) :] = jnp.zeros((BLK, width), jnp.float32)


def factor(matrix, want_low):
    order = matrix.shape[0]
    whole = pl.BlockSpec(memory_space=pltpu.VMEM)
    count = 2 if want_low else 1
    return pl.pallas_call(
        functools.partial(factor_kernel, order // BLK, want_low),
        out_shape=[jax.ShapeDtypeStruct((order, order), jnp.float32)] * count,
        in_specs=[whole],
        out_specs=[whole] * count,
        scratch_shapes=[pltpu.VMEM((BLK, order), jnp.float32)],
        cost_estimate=pl.CostEstimate(
            flops=40 * 1000**3, bytes_accessed=12 * order * order, transcendentals=0
        ),
        compiler_params=pltpu.CompilerParams(vmem_limit_bytes=24 << 20),
        name="factor_low" if want_low else "factor",
    )(matrix)


def schur_kernel(step_blocks, present_ref, absent_ref, rows_ref, high_ref, low_ref, out_ref, buf, zero, sem, zsem):
    step = pl.program_id(0)
    steps = pl.num_programs(0)
    slot = lax.rem(step, 2)

    def put(which, index, to):
        return pltpu.make_async_copy(
            buf.at[which, pl.ds(index * BLK, BLK)],
            out_ref.at[pl.ds(pl.multiple_of(to * BLK, BLK), BLK)],
            sem.at[which, index],
        )

    def clear(index, to):
        return pltpu.make_async_copy(
            zero, out_ref.at[pl.ds(pl.multiple_of(to * BLK, BLK), BLK)], zsem.at[index]
        )

    @pl.when(step == 0)
    def _():
        zero[...] = jnp.zeros_like(zero)

    for i in range(step_blocks):
        clear(i, absent_ref[step * step_blocks + i]).start()
    x = rows_ref[...]
    xh = x.astype(jnp.bfloat16)
    xl = (x - xh.astype(jnp.float32)).astype(jnp.bfloat16)
    wh = high_ref[...]
    total = jnp.dot(xh, wh, preferred_element_type=jnp.float32)
    total += jnp.dot(xh, low_ref[...], preferred_element_type=jnp.float32)
    total += jnp.dot(xl, wh, preferred_element_type=jnp.float32)

    @pl.when(step >= 2)
    def _():
        for i in range(step_blocks):
            put(slot, i, 0).wait()

    buf[slot] = total
    for i in range(step_blocks):
        put(slot, i, present_ref[step * step_blocks + i]).start()
    for i in range(step_blocks):
        clear(i, 0).wait()

    @pl.when(step == steps - 1)
    def _():
        for i in range(step_blocks):
            put(slot, i, 0).wait()
            put(1 - slot, i, 0).wait()


def schur_slab(present, absent, rows, high, low, step_blocks=4):
    width = high.shape[1]
    steps = SBLK // step_blocks
    return pl.pallas_call(
        functools.partial(schur_kernel, step_blocks),
        out_shape=jax.ShapeDtypeStruct((PBLK * BLK, width), jnp.float32),
        grid_spec=pltpu.PrefetchScalarGridSpec(
            num_scalar_prefetch=2,
            grid=(steps,),
            in_specs=[
                pl.BlockSpec((step_blocks * BLK, PIV), lambda i, p, a: (i, 0)),
                pl.BlockSpec((PIV, width), lambda i, p, a: (0, 0)),
                pl.BlockSpec((PIV, width), lambda i, p, a: (0, 0)),
            ],
            out_specs=pl.BlockSpec(memory_space=pl.ANY),
            scratch_shapes=[
                pltpu.VMEM((2, step_blocks * BLK, width), jnp.float32),
                pltpu.VMEM((BLK, width), jnp.float32),
                pltpu.SemaphoreType.DMA((2, step_blocks)),
                pltpu.SemaphoreType.DMA((step_blocks,)),
            ],
        ),
        cost_estimate=pl.CostEstimate(
            flops=6 * SBLK * BLK * PIV * width, bytes_accessed=36 << 20, transcendentals=0
        ),
        compiler_params=pltpu.CompilerParams(
            dimension_semantics=("arbitrary",), vmem_limit_bytes=32 << 20
        ),
        name="schur",
    )(present, absent, rows, high, low)


def swap_core(x):
    return lax.ppermute(x, "grp", [(i, i ^ 1) for i in range(8)])


def along_z(x, shift):
    return lax.ppermute(x, "grp", [(i, (i + 2 * shift) % 8) for i in range(8)])


def along_x(x, shift):
    return lax.ppermute(x, "col", [(i, (i + 4 * shift) % 16) for i in range(16)])


def along_y(x, shift):
    return lax.ppermute(x, "col", [(i, i // 4 * 4 + (i + shift) % 4) for i in range(16)])


def spread(x, mover, here):
    parts = [x] + [mover(x, s) for s in (1, 2, 3)]
    stacked = jnp.stack(parts)
    order = (here - jnp.arange(4, dtype=jnp.int32)) % 4
    return jnp.take(stacked, order, axis=0)


def gather_plane(x, px, py):
    half = x.shape[0] // 2
    first, second = x[:half], x[half:]
    first = spread(first, along_y, py)
    second = spread(second, along_x, px)
    first = spread(first, along_x, px)
    second = spread(second, along_y, py)
    second = second.transpose(1, 0, 2, 3)
    both = jnp.concatenate([first, second], axis=2)
    return both.reshape(16, *x.shape)


def pick(x, index, axis):
    return lax.dynamic_index_in_dim(x, index, axis, keepdims=False)


def sum_small(x, core):
    halves = x.reshape(2, x.shape[0] // 2, x.shape[1])
    got = swap_core(pick(halves, 1 - core, 0))
    mine = pick(halves, core, 0) + got
    mine = mine + along_z(mine, 1) + along_z(mine, 2) + along_z(mine, 3)
    other = swap_core(mine)
    lowest = jnp.where(core == 0, mine, other)
    highest = jnp.where(core == 0, other, mine)
    return jnp.concatenate([lowest, highest], axis=0)


def scatter_sum(x, pz, core):
    halves = x.reshape(2, x.shape[0] // 2, x.shape[1])
    got = swap_core(pick(halves, 1 - core, 0))
    mine = (pick(halves, core, 0) + got).reshape(4, -1, x.shape[1])
    total = pick(mine, pz, 0)
    for s in (1, 2, 3):
        total = total + along_z(pick(mine, (pz + s) % 4, 0), s)
    return total


def gather_grp(x, pz, core):
    mine = spread(x, along_z, pz).reshape(-1, x.shape[1])
    other = swap_core(mine)
    lowest = jnp.where(core == 0, mine, other)
    highest = jnp.where(core == 0, other, mine)
    return jnp.concatenate([lowest, highest], axis=0)


def high_dot(a, b, ca=1, cb=0):
    return lax.dot_general(
        a, b, (((ca,), (cb,)), ((), ())), precision=HIGH, preferred_element_type=jnp.float32
    )


def per_device(pivot_blocks, coupling, block_map, parent_matrix):
    g = lax.axis_index("grp")
    c = lax.axis_index("col")
    pz, core = g // 2, g % 2
    px, py = c // 4, c % 4
    at_top = g == 0

    gathered = lax.all_gather(coupling[0], "col", axis=0, tiled=True)

    lead_own = jnp.zeros((PANEL, BLK), jnp.float32)
    for s in range(8):
        piece = parent_matrix[PANEL * (s % 2) : PANEL * (s % 2) + PANEL, BLK * (s // 2) : BLK * (s // 2) + BLK]
        lead_own = lead_own + lax.ppermute(piece, "col", [(0, s), (1, 8 + s)])
    lead_own = jnp.where(at_top, lead_own, 0.0)

    mapping = pick(block_map, g, 0)
    spots = jnp.arange(PBLK, dtype=jnp.int32)
    matches = mapping[None, :] == spots[:, None]
    position = jnp.sum(jnp.where(matches, jnp.arange(SBLK, dtype=jnp.int32)[None, :], 0), axis=1)
    present = jnp.any(matches, axis=1)
    rank = jnp.sum((spots[None, :] < spots[:, None]) & ~present[None, :], axis=1)
    slots = jnp.arange(SBLK, dtype=jnp.int32)
    absent = jnp.sum(
        jnp.where((rank[None, :] == slots[:, None]) & ~present[None, :], spots[None, :], 0), axis=1
    ).astype(jnp.int32)

    (child_inv,) = factor(pivot_blocks[0], False)
    child_rows = high_dot(coupling[0], child_inv, 1, 1)

    def block(spot):
        where = position[spot]
        rows = lax.dynamic_slice_in_dim(gathered, where * BLK, BLK, 0)
        return jnp.where(present[spot], rows, 0.0)

    wanted = jnp.concatenate([block(4 * c + i) for i in range(4)] + [block(c // 2)], axis=0)
    half_way = high_dot(child_inv, wanted, 1, 1)
    solved = -high_dot(child_inv, half_way, 0, 0)

    first = high_dot(gathered[: MOSTR * BLK], solved)
    tiles = first.reshape(MOSTR, BLK, -1)
    top = jnp.concatenate(
        [
            jnp.where(present[r], pick(tiles, jnp.minimum(position[r], MOSTR - 1), 0), 0.0)
            for r in range(RBK)
        ],
        axis=0,
    )
    lead_part = lax.dynamic_slice(top, (PANEL * (c % 2), jnp.int32(PANEL)), (PANEL, BLK)) + lead_own
    lead_piece = sum_small(lead_part, core)
    lead_all = gather_plane(lead_piece, px, py)
    lead = lead_all.reshape(8, LEAD, BLK).transpose(1, 0, 2).reshape(LEAD, LEAD)
    lead_inv, lead_low = factor(lead, True)

    top_part = top[:, :PANEL] + jnp.where(at_top, parent_matrix, 0.0)
    slab = scatter_sum(top_part, pz, core)
    mine_top = gather_grp(slab, pz, core)
    turn = [
        (gg * 16 + cc, (cc // 2) * 16 + 2 * gg + cc % 2) for gg in range(8) for cc in range(16)
    ]
    turned = lax.ppermute(slab, ("grp", "col"), turn)
    around = gather_plane(turned, px, py)
    by_grp = around.reshape(4, 2, 2, BLK, PANEL)
    own_rows = by_grp.transpose(1, 0, 3, 2, 4).reshape(LEAD, LEAD)

    width = solved[:, :PANEL]
    wide_high = lax.reduce_precision(width, 8, 7)
    solved_high = wide_high.astype(jnp.bfloat16)
    solved_low = (width - wide_high).astype(jnp.bfloat16)
    slab_all = schur_slab(mapping, absent, gathered, solved_high, solved_low)
    update = lax.psum_scatter(slab_all, "grp", scatter_dimension=0, tiled=True)
    assembled = parent_matrix + update

    forward = high_dot(lead_inv, mine_top)
    back = high_dot(lead_inv, forward, 0, 0)
    in_panel = c < 2
    column = PANEL * jnp.minimum(c, 1)

    def below(_):
        turned_inv = lax.dynamic_slice(lead_inv, (column, jnp.int32(0)), (PANEL, LEAD)).T
        factor_cols = jnp.where(in_panel, -turned_inv, back)
        start = jnp.where(in_panel, 0.0, assembled)
        return start - high_dot(own_rows, factor_cols, 0, 0)

    def leading(_):
        panel_cols = lax.dynamic_slice(lead_low, (jnp.int32(0), column), (LEAD, PANEL))
        lower = assembled[PANEL:] - high_dot(lead_low[PANEL:, :PANEL], forward[:PANEL])
        upper = jnp.where(c == 0, panel_cols[:PANEL], assembled[:PANEL])
        lower = jnp.where(in_panel, panel_cols[PANEL:], lower)
        return jnp.concatenate([upper, lower], axis=0)

    matrix = lax.cond(at_top, leading, below, 0)
    return (child_rows[None], matrix)


def solution(mesh):
    return jax.shard_map(
        per_device,
        mesh=mesh,
        in_specs=(P("grp", None, None), P("grp", "col", None), P(), P("grp", "col")),
        out_specs=(P("grp", "col", None), P("grp", "col")),
        check_vma=False,
    )
```

```python
import functools

import jax
import jax.numpy as jnp
from jax import lax
from jax.experimental import pallas as pl
from jax.experimental.pallas import tpu as pltpu
from jax.sharding import PartitionSpec as P


BLK = 128
PANEL = 512
LEAD = 1024
PIV = 1024
SBLK = 32
PBLK = 64
RBK = 8

HIGHEST = lax.Precision.HIGHEST
HIGH = lax.Precision.HIGH


def eliminate(work):
    order = BLK
    lane = lax.broadcasted_iota(jnp.int32, (8, order), 1)
    sub = lax.broadcasted_iota(jnp.int32, (8, order), 0)
    parts = order // 8
    rows = [work[8 * q : 8 * q + 8, :] for q in range(parts)]
    low = [jnp.zeros((8, order), jnp.float32) for _ in range(parts)]
    for q in range(parts):
        cols = [
            [
                jnp.broadcast_to(rows[p][:, 8 * q + k : 8 * q + k + 1], (8, order))
                for p in range(q, parts)
            ]
            for k in range(8)
        ]
        here = (lane >= 8 * q) & (lane < 8 * q + 8)
        mine = jnp.where(here, jnp.where(lane == sub + 8 * q, 1.0, 0.0), rows[q])
        fresh = []
        for k in range(8):
            root = lax.rsqrt(jnp.broadcast_to(cols[k][0][k : k + 1, :], (8, order)))
            cols[k] = [c * root for c in cols[k]]
            cols[k][0] = jnp.where(sub >= k, cols[k][0], 0.0)
            for m in range(k + 1, 8):
                scale = jnp.broadcast_to(cols[k][0][m : m + 1, :], (8, order))
                cols[m] = [a - b * scale for a, b in zip(cols[m], cols[k])]
            scaled = mine * root
            row = jnp.broadcast_to(scaled[k : k + 1, :], (8, order))
            fresh.append(row)
            mine = jnp.where(sub > k, mine - cols[k][0] * row, jnp.where(sub == k, scaled, mine))
        rows[q] = mine
        for p in range(q, parts):
            for k in range(8):
                low[p] = jnp.where(lane == 8 * q + k, cols[k][p - q], low[p])
        for p in range(q + 1, parts):
            acc = jnp.where(here, 0.0, rows[p])
            for k in range(8):
                acc = acc - cols[k][p - q] * fresh[k]
            rows[p] = acc
    for q in range(parts):
        rows[q] = jnp.where(lane <= sub + 8 * q, rows[q], 0.0)
    return jnp.concatenate(rows, axis=0), jnp.concatenate(low, axis=0)


def exact(a, b):
    return jnp.dot(a, b, precision=HIGHEST, preferred_element_type=jnp.float32)


def factor_kernel(blocks, want_low, a_ref, *refs):
    if want_low:
        t_ref, l_ref, r_ref = refs
    else:
        t_ref, r_ref = refs
    order = blocks * BLK
    t_ref[...] = a_ref[...]

    def step(b, carry):
        at = pl.multiple_of(b * BLK, BLK)
        inv, low = eliminate(t_ref[pl.ds(at, BLK), pl.ds(at, BLK)])
        r_ref[...] = exact(inv, t_ref[pl.ds(at, BLK), :])
        r_ref[:, pl.ds(at, BLK)] = inv
        t_ref[pl.ds(at, BLK), :] = r_ref[...]
        if want_low:
            l_ref[:, pl.ds(at, BLK)] = jnp.zeros((order, BLK), jnp.float32)
            l_ref[pl.ds(at, BLK), pl.ds(at, BLK)] = low

        def below(i, carry):
            to = pl.multiple_of(i * BLK, BLK)
            left = r_ref[:, pl.ds(to, BLK)].T
            if want_low:
                l_ref[pl.ds(to, BLK), pl.ds(at, BLK)] = left
            t_ref[pl.ds(to, BLK), pl.ds(at, BLK)] = jnp.zeros((BLK, BLK), jnp.float32)
            t_ref[pl.ds(to, BLK), :] = t_ref[pl.ds(to, BLK), :] - exact(left, r_ref[...])
            return carry

        return lax.fori_loop(b + 1, blocks, below, carry)

    lax.fori_loop(0, blocks, step, 0)
    for b in range(blocks - 1):
        width = order - BLK * (b + 1)
        t_ref[BLK * b : BLK * b + BLK, BLK * (b + 1) :] = jnp.zeros((BLK, width), jnp.float32)


def factor(matrix, want_low):
    order = matrix.shape[0]
    whole = pl.BlockSpec(memory_space=pltpu.VMEM)
    count = 2 if want_low else 1
    return pl.pallas_call(
        functools.partial(factor_kernel, order // BLK, want_low),
        out_shape=[jax.ShapeDtypeStruct((order, order), jnp.float32)] * count,
        in_specs=[whole],
        out_specs=[whole] * count,
        scratch_shapes=[pltpu.VMEM((BLK, order), jnp.float32)],
        cost_estimate=pl.CostEstimate(
            flops=40 * 1000**3, bytes_accessed=12 * order * order, transcendentals=0
        ),
        compiler_params=pltpu.CompilerParams(vmem_limit_bytes=24 << 20),
        name="factor_low" if want_low else "factor",
    )(matrix)


def schur_kernel(step_blocks, present_ref, absent_ref, rows_ref, high_ref, low_ref, out_ref, buf, zero, sem, zsem):
    step = pl.program_id(0)
    steps = pl.num_programs(0)
    slot = lax.rem(step, 2)

    def put(which, index, to):
        return pltpu.make_async_copy(
            buf.at[which, pl.ds(index * BLK, BLK)],
            out_ref.at[pl.ds(pl.multiple_of(to * BLK, BLK), BLK)],
            sem.at[which, index],
        )

    def clear(index, to):
        return pltpu.make_async_copy(
            zero, out_ref.at[pl.ds(pl.multiple_of(to * BLK, BLK), BLK)], zsem.at[index]
        )

    @pl.when(step == 0)
    def _():
        zero[...] = jnp.zeros_like(zero)

    for i in range(step_blocks):
        clear(i, absent_ref[step * step_blocks + i]).start()
    x = rows_ref[...]
    xh = x.astype(jnp.bfloat16)
    xl = (x - xh.astype(jnp.float32)).astype(jnp.bfloat16)
    wh = high_ref[...]
    total = jnp.dot(xh, wh, preferred_element_type=jnp.float32)
    total += jnp.dot(xh, low_ref[...], preferred_element_type=jnp.float32)
    total += jnp.dot(xl, wh, preferred_element_type=jnp.float32)

    @pl.when(step >= 2)
    def _():
        for i in range(step_blocks):
            put(slot, i, 0).wait()

    buf[slot] = total
    for i in range(step_blocks):
        put(slot, i, present_ref[step * step_blocks + i]).start()
    for i in range(step_blocks):
        clear(i, 0).wait()

    @pl.when(step == steps - 1)
    def _():
        for i in range(step_blocks):
            put(slot, i, 0).wait()
            put(1 - slot, i, 0).wait()


def schur_slab(present, absent, rows, high, low, step_blocks=4):
    width = high.shape[1]
    steps = SBLK // step_blocks
    return pl.pallas_call(
        functools.partial(schur_kernel, step_blocks),
        out_shape=jax.ShapeDtypeStruct((PBLK * BLK, width), jnp.float32),
        grid_spec=pltpu.PrefetchScalarGridSpec(
            num_scalar_prefetch=2,
            grid=(steps,),
            in_specs=[
                pl.BlockSpec((step_blocks * BLK, PIV), lambda i, p, a: (i, 0)),
                pl.BlockSpec((PIV, width), lambda i, p, a: (0, 0)),
                pl.BlockSpec((PIV, width), lambda i, p, a: (0, 0)),
            ],
            out_specs=pl.BlockSpec(memory_space=pltpu.HBM),
            scratch_shapes=[
                pltpu.VMEM((2, step_blocks * BLK, width), jnp.float32),
                pltpu.VMEM((BLK, width), jnp.float32),
                pltpu.SemaphoreType.DMA((2, step_blocks)),
                pltpu.SemaphoreType.DMA((step_blocks,)),
            ],
        ),
        cost_estimate=pl.CostEstimate(
            flops=6 * SBLK * BLK * PIV * width, bytes_accessed=36 << 20, transcendentals=0
        ),
        compiler_params=pltpu.CompilerParams(
            dimension_semantics=("arbitrary",), vmem_limit_bytes=58 << 20
        ),
        name="schur",
    )(present, absent, rows, high, low)


def choose_kernel(where_ref, there_ref, rows_ref, out_ref):
    there = there_ref[pl.program_id(0)] > 0
    out_ref[...] = jnp.where(there, rows_ref[...], 0.0)


def choose(where, there, rows):
    count = where.shape[0]
    return pl.pallas_call(
        choose_kernel,
        out_shape=jax.ShapeDtypeStruct((count * BLK, PIV), jnp.float32),
        grid_spec=pltpu.PrefetchScalarGridSpec(
            num_scalar_prefetch=2,
            grid=(count,),
            in_specs=[pl.BlockSpec((BLK, PIV), lambda i, w, t: (w[i], 0))],
            out_specs=pl.BlockSpec((BLK, PIV), lambda i, w, t: (i, 0)),
        ),
        cost_estimate=pl.CostEstimate(
            flops=0, bytes_accessed=8 * count * BLK * PIV, transcendentals=0
        ),
        name="choose",
    )(where, there, rows)


def swap_core(x):
    return lax.ppermute(x, "grp", [(i, i ^ 1) for i in range(8)])


def along_z(x, shift):
    return lax.ppermute(x, "grp", [(i, (i + 2 * shift) % 8) for i in range(8)])


def along_x(x, shift):
    return lax.ppermute(x, "col", [(i, (i + 4 * shift) % 16) for i in range(16)])


def along_y(x, shift):
    return lax.ppermute(x, "col", [(i, i // 4 * 4 + (i + shift) % 4) for i in range(16)])


def fetch(x, mover):
    return jnp.stack([x] + [mover(x, s) for s in (1, 2, 3)])


def ordered(stacked, here):
    order = (here - jnp.arange(4, dtype=jnp.int32)) % 4
    return jnp.take(stacked, order, axis=0, mode="clip")


def plane_near(x):
    half = x.shape[0] // 2
    return fetch(x[:half], along_y), fetch(x[half:], along_x)


def plane_far(near):
    return fetch(near[0], along_x), fetch(near[1], along_y)


def plane_order(far, px, py):
    slots = jnp.arange(16, dtype=jnp.int32)
    rel_x, rel_y = (px - slots // 4) % 4, (py - slots % 4) % 4
    first = far[0].reshape(16, *far[0].shape[2:])
    second = far[1].reshape(16, *far[1].shape[2:])
    first = jnp.take(first, rel_x * 4 + rel_y, axis=0, mode="clip")
    second = jnp.take(second, rel_y * 4 + rel_x, axis=0, mode="clip")
    return jnp.concatenate([first, second], axis=1)


def pick(x, index, axis):
    return lax.dynamic_index_in_dim(x, index, axis, keepdims=False)


def join_cores(mine, other, core):
    lowest = jnp.where(core == 0, mine, other)
    highest = jnp.where(core == 0, other, mine)
    return jnp.concatenate([lowest, highest], axis=0)


def high_dot(a, b, ca=1, cb=0):
    return lax.dot_general(
        a, b, (((ca,), (cb,)), ((), ())), precision=HIGH, preferred_element_type=jnp.float32
    )


def after(value, *others):
    return lax.optimization_barrier((value, *others))[0]


def program(pivot_blocks, coupling, block_map, parent_matrix):
    g = lax.axis_index("grp")
    c = lax.axis_index("col")
    pz, core = g // 2, g % 2
    px, py = c // 4, c % 4
    at_top = g == 0

    gathered = lax.all_gather(coupling[0], "col", axis=0, tiled=True)

    lead_own = jnp.zeros((PANEL, BLK), jnp.float32)
    for s in range(8):
        row, column = PANEL * (s % 2), BLK * (s // 2)
        piece = parent_matrix[row : row + PANEL, column : column + BLK]
        lead_own = lead_own + lax.ppermute(piece, "col", [(0, s), (1, 8 + s)])
    lead_own = jnp.where(at_top, lead_own, 0.0)

    mapping = pick(block_map, g, 0)
    spots = jnp.arange(PBLK, dtype=jnp.int32)
    matches = mapping[None, :] == spots[:, None]
    position = jnp.sum(jnp.where(matches, jnp.arange(SBLK, dtype=jnp.int32)[None, :], 0), axis=1)
    present = jnp.any(matches, axis=1)
    rank = jnp.sum((spots[None, :] < spots[:, None]) & ~present[None, :], axis=1)
    slots = jnp.arange(SBLK, dtype=jnp.int32)
    absent = jnp.sum(
        jnp.where((rank[None, :] == slots[:, None]) & ~present[None, :], spots[None, :], 0), axis=1
    ).astype(jnp.int32)
    picks = jnp.arange(13, dtype=jnp.int32)
    spot = jnp.where(picks < 8, picks, jnp.where(picks < 12, 4 * c + picks - 8, c // 2))
    chosen = spot[:, None] == spots[None, :]
    where = jnp.sum(jnp.where(chosen, position[None, :], 0), axis=1)
    there = jnp.sum((chosen & present[None, :]).astype(jnp.int32), axis=1)

    pivot, lead_own, where, there, absent = lax.optimization_barrier(
        (pivot_blocks[0], lead_own, where, there, absent)
    )
    (child_inv,) = factor(pivot, False)
    child_rows = high_dot(coupling[0], child_inv, 1, 1)
    gathered, child_rows = lax.optimization_barrier((gathered, child_rows))

    blocks = choose(where, there, gathered)
    half_way = high_dot(child_inv, blocks[RBK * BLK :], 1, 1)
    solved = -high_dot(child_inv, half_way, 0, 0)

    top = high_dot(blocks[: RBK * BLK], solved)
    lead_part = lax.dynamic_slice(top, (PANEL * (c % 2), jnp.int32(PANEL)), (PANEL, BLK)) + lead_own
    top_part = top[:, :PANEL] + jnp.where(at_top, parent_matrix, 0.0)

    lead_halves = lead_part.reshape(2, PANEL // 2, BLK)
    top_halves = top_part.reshape(2, PANEL, PANEL)
    lead_got = swap_core(pick(lead_halves, 1 - core, 0))
    top_got = swap_core(pick(top_halves, 1 - core, 0))
    lead_mine = pick(lead_halves, core, 0) + lead_got
    others = [along_z(lead_mine, s) for s in (1, 2, 3)]

    width = solved[:, :PANEL]
    wide_high = lax.reduce_precision(width, 8, 7)
    solved_high = wide_high.astype(jnp.bfloat16)
    solved_low = (width - wide_high).astype(jnp.bfloat16)
    slab_all = schur_slab(mapping, absent, after(gathered, lead_got), solved_high, solved_low)
    update = lax.psum_scatter(slab_all, "grp", scatter_dimension=0, tiled=True)

    lead_mine = lead_mine + others[0] + others[1] + others[2]
    lead_piece = join_cores(lead_mine, swap_core(lead_mine), core)

    top_mine = (pick(top_halves, core, 0) + top_got).reshape(4, BLK, PANEL)
    top_mine = after(top_mine, lead_mine)
    strip = pick(top_mine, pz, 0)
    for s in (1, 2, 3):
        strip = strip + along_z(pick(top_mine, (pz + s) % 4, 0), s)

    lead_near = plane_near(lead_piece)
    strip = after(strip, lead_near)
    turn = [
        (gg * 16 + cc, (cc // 2) * 16 + 2 * gg + cc % 2) for gg in range(8) for cc in range(16)
    ]
    turned = lax.ppermute(strip, ("grp", "col"), turn)
    lead_far = plane_far(lead_near)
    row_near = plane_near(turned)
    lead_far, row_near = lax.optimization_barrier((lead_far, row_near))
    row_far = plane_far(row_near)
    top_four = fetch(after(strip, lead_far), along_z)
    lead_all = plane_order(lead_far, px, py)
    lead = lead_all.reshape(8, LEAD, BLK).transpose(1, 0, 2).reshape(LEAD, LEAD)
    lead_inv, lead_low = factor(lead, True)

    top_rows = ordered(top_four, pz).reshape(PANEL, PANEL)
    mine_top = join_cores(top_rows, swap_core(top_rows), core)
    around = plane_order(row_far, px, py)
    by_grp = around.reshape(4, 2, 2, BLK, PANEL)
    own_rows = by_grp.transpose(1, 0, 3, 2, 4).reshape(LEAD, LEAD)

    forward = high_dot(lead_inv, mine_top)
    back = high_dot(lead_inv, forward, 0, 0)
    assembled = after(parent_matrix, lead_inv) + update
    in_panel = c < 2
    column = PANEL * jnp.minimum(c, 1)

    def below(_):
        turned_inv = lax.dynamic_slice(lead_inv, (column, jnp.int32(0)), (PANEL, LEAD)).T
        factor_cols = jnp.where(in_panel, -turned_inv, back)
        start = jnp.where(in_panel, 0.0, assembled)
        return start - high_dot(own_rows, factor_cols, 0, 0)

    def leading(_):
        panel_cols = lax.dynamic_slice(lead_low, (jnp.int32(0), column), (LEAD, PANEL))
        lower = assembled[PANEL:] - high_dot(lead_low[PANEL:, :PANEL], forward[:PANEL])
        upper = jnp.where(c == 0, panel_cols[:PANEL], assembled[:PANEL])
        lower = jnp.where(in_panel, panel_cols[PANEL:], lower)
        return jnp.concatenate([upper, lower], axis=0)

    matrix = lax.cond(at_top, leading, below, 0)
    return (child_rows[None], matrix)


def solution(mesh):
    return jax.shard_map(
        program,
        mesh=mesh,
        in_specs=(P("grp", None, None), P("grp", "col", None), P(), P("grp", "col")),
        out_specs=(P("grp", "col", None), P("grp", "col")),
        check_vma=False,
    )
```

```python
import functools

import jax
import jax.numpy as jnp
from jax import lax
from jax.experimental import pallas as pl
from jax.experimental.pallas import tpu as pltpu
from jax.sharding import PartitionSpec as P


BLK = 128
PANEL = 512
LEAD = 1024
PIV = 1024
SBLK = 32
PBLK = 64

HIGHEST = lax.Precision.HIGHEST


def eliminate(work):
    order = BLK
    lane = lax.broadcasted_iota(jnp.int32, (8, order), 1)
    sub = lax.broadcasted_iota(jnp.int32, (8, order), 0)
    parts = order // 8
    rows = [work[8 * q : 8 * q + 8, :] for q in range(parts)]
    low = [jnp.zeros((8, order), jnp.float32) for _ in range(parts)]
    for q in range(parts):
        cols = [
            [
                jnp.broadcast_to(rows[p][:, 8 * q + k : 8 * q + k + 1], (8, order))
                for p in range(q, parts)
            ]
            for k in range(8)
        ]
        here = (lane >= 8 * q) & (lane < 8 * q + 8)
        mine = jnp.where(here, jnp.where(lane == sub + 8 * q, 1.0, 0.0), rows[q])
        fresh = []
        for k in range(8):
            root = lax.rsqrt(jnp.broadcast_to(cols[k][0][k : k + 1, :], (8, order)))
            cols[k] = [c * root for c in cols[k]]
            cols[k][0] = jnp.where(sub >= k, cols[k][0], 0.0)
            for m in range(k + 1, 8):
                scale = jnp.broadcast_to(cols[k][0][m : m + 1, :], (8, order))
                cols[m] = [a - b * scale for a, b in zip(cols[m], cols[k])]
            scaled = mine * root
            row = jnp.broadcast_to(scaled[k : k + 1, :], (8, order))
            fresh.append(row)
            mine = jnp.where(sub > k, mine - cols[k][0] * row, jnp.where(sub == k, scaled, mine))
        rows[q] = mine
        for p in range(q, parts):
            for k in range(8):
                low[p] = jnp.where(lane == 8 * q + k, cols[k][p - q], low[p])
        for p in range(q + 1, parts):
            acc = jnp.where(here, 0.0, rows[p])
            for k in range(8):
                acc = acc - cols[k][p - q] * fresh[k]
            rows[p] = acc
    for q in range(parts):
        rows[q] = jnp.where(lane <= sub + 8 * q, rows[q], 0.0)
    return jnp.concatenate(rows, axis=0), jnp.concatenate(low, axis=0)


def exact(a, b):
    return jnp.dot(a, b, precision=HIGHEST, preferred_element_type=jnp.float32)


def factor_steps(first, last, t_ref, l_ref, r_ref):
    order = t_ref.shape[0]
    blocks = order // BLK

    def step(b, carry):
        at = pl.multiple_of(b * BLK, BLK)
        inv, low = eliminate(t_ref[pl.ds(at, BLK), pl.ds(at, BLK)])
        r_ref[...] = exact(inv, t_ref[pl.ds(at, BLK), :])
        r_ref[:, pl.ds(at, BLK)] = inv
        t_ref[pl.ds(at, BLK), :] = r_ref[...]
        if l_ref is not None:
            l_ref[:, pl.ds(at, BLK)] = jnp.zeros((order, BLK), jnp.float32)
            l_ref[pl.ds(at, BLK), pl.ds(at, BLK)] = low

        def below(i, carry):
            to = pl.multiple_of(i * BLK, BLK)
            left = r_ref[:, pl.ds(to, BLK)].T
            if l_ref is not None:
                l_ref[pl.ds(to, BLK), pl.ds(at, BLK)] = left
            t_ref[pl.ds(to, BLK), pl.ds(at, BLK)] = jnp.zeros((BLK, BLK), jnp.float32)
            t_ref[pl.ds(to, BLK), :] = t_ref[pl.ds(to, BLK), :] - exact(left, r_ref[...])
            return carry

        return lax.fori_loop(b + 1, blocks, below, carry)

    lax.fori_loop(first, last, step, 0)
    if last == blocks:
        for b in range(blocks - 1):
            width = order - BLK * (b + 1)
            t_ref[BLK * b : BLK * b + BLK, BLK * (b + 1) :] = jnp.zeros((BLK, width), jnp.float32)


def child_kernel(a_ref, t_ref, r_ref):
    t_ref[...] = a_ref[...]
    factor_steps(0, PIV // BLK, t_ref, None, r_ref)


def lead_start_kernel(last, place_ref, *refs):
    pieces, (t_ref, l_ref, r_ref) = refs[:8], refs[8:]
    px, py = place_ref[0], place_ref[1]
    for sx in range(4):
        for sy in range(4):
            x, y = (px + 4 - sx) % 4, (py + 4 - sy) % 4
            where = x * 4 + y
            row = pl.multiple_of((where % 2) * PANEL, PANEL)
            column = pl.multiple_of((where // 2) * BLK, BLK)
            t_ref[pl.ds(row, PANEL // 2), pl.ds(column, BLK)] = pieces[sx][sy]
            t_ref[pl.ds(row + PANEL // 2, PANEL // 2), pl.ds(column, BLK)] = pieces[4 + sy][sx]
    factor_steps(0, last, t_ref, l_ref, r_ref)


def lead_next_kernel(first, last, t_in, l_in, t_ref, l_ref, r_ref):
    factor_steps(first, last, t_ref, l_ref, r_ref)


WHOLE = pl.BlockSpec(memory_space=pltpu.VMEM)
TABLE = pl.BlockSpec(memory_space=pltpu.SMEM)


def square(order):
    return jax.ShapeDtypeStruct((order, order), jnp.float32)


def limit(mib):
    return pltpu.CompilerParams(vmem_limit_bytes=mib << 20)


def work(gflop, mib):
    return pl.CostEstimate(
        flops=int(gflop * 10**9), bytes_accessed=mib << 20, transcendentals=0
    )


def child_factor(matrix):
    return pl.pallas_call(
        child_kernel,
        out_shape=square(PIV),
        in_specs=[WHOLE],
        out_specs=WHOLE,
        scratch_shapes=[pltpu.VMEM((BLK, PIV), jnp.float32)],
        cost_estimate=work(40, 12),
        compiler_params=limit(24),
        name="child_factor",
    )(matrix)


def lead_start(place, pieces, last):
    return pl.pallas_call(
        functools.partial(lead_start_kernel, last),
        out_shape=[square(LEAD)] * 2,
        in_specs=[TABLE] + [WHOLE] * 8,
        out_specs=[WHOLE] * 2,
        scratch_shapes=[pltpu.VMEM((BLK, LEAD), jnp.float32)],
        cost_estimate=work(10, 12),
        compiler_params=limit(24),
        name="lead_start",
    )(place, *pieces)


def lead_next(t, l, first, last):
    return pl.pallas_call(
        functools.partial(lead_next_kernel, first, last),
        out_shape=[square(LEAD)] * 2,
        in_specs=[WHOLE] * 2,
        out_specs=[WHOLE] * 2,
        input_output_aliases={0: 0, 1: 1},
        scratch_shapes=[pltpu.VMEM((BLK, LEAD), jnp.float32)],
        cost_estimate=work(10, 12),
        compiler_params=limit(24),
        name="lead_next",
    )(t, l)


def split(x):
    high = x.astype(jnp.bfloat16)
    return high, (x - high.astype(jnp.float32)).astype(jnp.bfloat16)


def product(a, b, turned=False):
    dims = (((1,), (1 if turned else 0,)), ((), ()))

    def one(x, y):
        return lax.dot_general(x, y, dims, preferred_element_type=jnp.float32)

    return one(a[0], b[0]) + one(a[0], b[1]) + one(a[1], b[0])


def rows_kernel(t_ref, c_ref, high_ref, low_ref, out_ref):
    high_ref[...], low_ref[...] = split(t_ref[...])
    out_ref[...] = product(split(c_ref[...]), (high_ref[...], low_ref[...]), True)


def child_rows_of(inverse, rows):
    half = jax.ShapeDtypeStruct((PIV, PIV), jnp.bfloat16)
    return pl.pallas_call(
        rows_kernel,
        out_shape=[half, half, jax.ShapeDtypeStruct(rows.shape, jnp.float32)],
        in_specs=[WHOLE] * 2,
        out_specs=[WHOLE] * 3,
        cost_estimate=work(2, 10),
        compiler_params=limit(32),
        name="child_rows",
    )(inverse, rows)


def load_blocks(count, where_ref, there_ref, rows_ref, got, sem):
    def copy(i):
        start = pl.multiple_of(where_ref[i] * BLK, BLK)
        return pltpu.make_async_copy(
            rows_ref.at[pl.ds(start, BLK)], got.at[pl.ds(i * BLK, BLK)], sem.at[i]
        )

    for i in range(count):
        copy(i).start()
    for i in range(count):
        copy(i).wait()

        @pl.when(there_ref[i] == 0)
        def _():
            got[i * BLK : i * BLK + BLK, :] = jnp.zeros((BLK, PIV), jnp.float32)


def lead_part_kernel(where_ref, there_ref, high_ref, low_ref, rows_ref, out_ref, got, sem):
    load_blocks(5, where_ref, there_ref, rows_ref, got, sem)
    inverse = (high_ref[...], low_ref[...])
    half_way = product(split(got[4 * BLK :, :]), inverse, True)
    solved = product(split(half_way), inverse)
    out_ref[...] = -product(split(got[: 4 * BLK, :]), split(solved), True)


def solved_kernel(where_ref, there_ref, high_ref, low_ref, rows_ref, oh_ref, ol_ref, got, sem):
    load_blocks(4, where_ref, there_ref, rows_ref, got, sem)
    inverse = (high_ref[...], low_ref[...])
    half_way = product(split(got[...]), inverse, True)
    solved = product(split(half_way), inverse)
    oh_ref[...], ol_ref[...] = split(-solved.T)


def with_blocks(kernel, count, out_shape, where, there, inverse, rows):
    many = isinstance(out_shape, list)
    return pl.pallas_call(
        kernel,
        out_shape=out_shape,
        in_specs=[TABLE] * 2 + [WHOLE] * 2 + [pl.BlockSpec(memory_space=pl.ANY)],
        out_specs=[WHOLE] * len(out_shape) if many else WHOLE,
        scratch_shapes=[
            pltpu.VMEM((count * BLK, PIV), jnp.float32),
            pltpu.SemaphoreType.DMA((count,)),
        ],
        cost_estimate=work(3, 8),
        compiler_params=limit(40),
    )(where, there, *inverse, rows)


def solve_kernel(
    place_ref, t_ref, low_ref, mine_ref, other_ref, *refs
):
    pieces, (out_ref, th, tl, uh, ul, ph, pl_, fh, fl, xh, xl, rh, rl) = refs[:8], refs[8:]
    g, c, pz, core, px, py = [place_ref[i] for i in range(6)]
    half = PANEL

    th[...], tl[...] = split(t_ref[...])
    for i in range(4):
        for j in range(4):
            rows = slice(256 * j, 256 * j + 256)
            cols = slice(256 * i, 256 * i + 256)
            uh[rows, cols], ul[rows, cols] = split(t_ref[cols, rows].T)
    for s in range(4):
        z = (pz + 4 - s) % 4
        at = pl.multiple_of(core * half + z * BLK, BLK)
        ph[pl.ds(at, BLK), :], pl_[pl.ds(at, BLK), :] = split(mine_ref[s])
        at = pl.multiple_of((1 - core) * half + z * BLK, BLK)
        ph[pl.ds(at, BLK), :], pl_[pl.ds(at, BLK), :] = split(other_ref[s])

    def tiles(count, body):
        def one(i, carry):
            body(pl.ds(pl.multiple_of(i * 256, 256), 256))
            return carry

        lax.fori_loop(0, count, one, 0)

    def forward(at):
        fh[at, :], fl[at, :] = split(product((th[at, :], tl[at, :]), (ph[...], pl_[...])))

    tiles(4, forward)

    @pl.when(g == 0)
    def _():
        @pl.when(c == 0)
        def _():
            out_ref[...] = -low_ref[:, :half]

        @pl.when(c == 1)
        def _():
            out_ref[:half, :] = jnp.zeros((half, half), jnp.float32)
            out_ref[half:, :] = -low_ref[half:, half:]

        @pl.when(c >= 2)
        def _():
            out_ref[:half, :] = jnp.zeros((half, half), jnp.float32)
            left = split(low_ref[half:, :half])
            out_ref[half:, :] = product(left, (fh[:half, :], fl[:half, :]))

    @pl.when(g > 0)
    def _():
        @pl.when(c == 0)
        def _():
            xh[...], xl[...] = -uh[:, :half], -ul[:, :half]

        @pl.when(c == 1)
        def _():
            xh[...], xl[...] = -uh[:, half:], -ul[:, half:]

        @pl.when(c >= 2)
        def _():
            def back(at):
                x = product((uh[at, :], ul[at, :]), (fh[...], fl[...]))
                xh[at, :], xl[at, :] = split(x)

            tiles(4, back)

        for sx in range(4):
            for sy in range(4):
                x, y = (px + 4 - sx) % 4, (py + 4 - sy) % 4
                where = x * 4 + y
                source = where // 2
                row = pl.multiple_of((where % 2) * half, half)
                column = pl.multiple_of(((source % 2) * 4 + source // 2) * BLK, BLK)
                tile = jnp.concatenate([pieces[sx][sy], pieces[4 + sy][sx]], axis=0).T
                to = (pl.ds(row, half), pl.ds(column, BLK))
                rh[to], rl[to] = split(tile)

        def update(at):
            out_ref[at, :] = product((rh[at, :], rl[at, :]), (xh[...], xl[...]))

        tiles(4, update)


def solve(place, inverse, low, mine, other, pieces):
    def pair(rows, cols):
        return [pltpu.VMEM((rows, cols), jnp.bfloat16)] * 2

    return pl.pallas_call(
        solve_kernel,
        out_shape=jax.ShapeDtypeStruct((LEAD, PANEL), jnp.float32),
        in_specs=[TABLE] + [WHOLE] * 12,
        out_specs=WHOLE,
        scratch_shapes=pair(LEAD, LEAD) * 2 + pair(LEAD, PANEL) * 3 + pair(LEAD, LEAD),
        cost_estimate=work(10, 20),
        compiler_params=limit(48),
        name="solve",
    )(place, inverse, low, mine, other, *pieces)


def schur_kernel(step_blocks, present_ref, absent_ref, rows_ref, high_ref, low_ref, out_ref, buf, zero, sem, zsem):
    step = pl.program_id(0)
    steps = pl.num_programs(0)
    slot = lax.rem(step, 2)

    def put(which, index, to):
        return pltpu.make_async_copy(
            buf.at[which, pl.ds(index * BLK, BLK)],
            out_ref.at[pl.ds(pl.multiple_of(to * BLK, BLK), BLK)],
            sem.at[which, index],
        )

    def clear(index, to):
        return pltpu.make_async_copy(
            zero, out_ref.at[pl.ds(pl.multiple_of(to * BLK, BLK), BLK)], zsem.at[index]
        )

    @pl.when(step == 0)
    def _():
        zero[...] = jnp.zeros_like(zero)

    for i in range(step_blocks):
        clear(i, absent_ref[step * step_blocks + i]).start()
    x = rows_ref[...]
    xh = x.astype(jnp.bfloat16)
    xl = (x - xh.astype(jnp.float32)).astype(jnp.bfloat16)
    wh = high_ref[...]
    total = jnp.dot(xh, wh, preferred_element_type=jnp.float32)
    total += jnp.dot(xh, low_ref[...], preferred_element_type=jnp.float32)
    total += jnp.dot(xl, wh, preferred_element_type=jnp.float32)

    @pl.when(step >= 2)
    def _():
        for i in range(step_blocks):
            put(slot, i, 0).wait()

    buf[slot] = total
    for i in range(step_blocks):
        put(slot, i, present_ref[step * step_blocks + i]).start()
    for i in range(step_blocks):
        clear(i, 0).wait()

    @pl.when(step == steps - 1)
    def _():
        for i in range(step_blocks):
            put(slot, i, 0).wait()
            put(1 - slot, i, 0).wait()


def schur_slab(present, absent, rows, high, low, step_blocks=4):
    width = high.shape[1]
    steps = SBLK // step_blocks
    return pl.pallas_call(
        functools.partial(schur_kernel, step_blocks),
        out_shape=jax.ShapeDtypeStruct((PBLK * BLK, width), jnp.float32),
        grid_spec=pltpu.PrefetchScalarGridSpec(
            num_scalar_prefetch=2,
            grid=(steps,),
            in_specs=[
                pl.BlockSpec((step_blocks * BLK, PIV), lambda i, p, a: (i, 0)),
                pl.BlockSpec((PIV, width), lambda i, p, a: (0, 0)),
                pl.BlockSpec((PIV, width), lambda i, p, a: (0, 0)),
            ],
            out_specs=pl.BlockSpec(memory_space=pltpu.HBM),
            scratch_shapes=[
                pltpu.VMEM((2, step_blocks * BLK, width), jnp.float32),
                pltpu.VMEM((BLK, width), jnp.float32),
                pltpu.SemaphoreType.DMA((2, step_blocks)),
                pltpu.SemaphoreType.DMA((step_blocks,)),
            ],
        ),
        cost_estimate=pl.CostEstimate(
            flops=6 * SBLK * BLK * PIV * width, bytes_accessed=36 << 20, transcendentals=0
        ),
        compiler_params=pltpu.CompilerParams(
            dimension_semantics=("arbitrary",), vmem_limit_bytes=58 << 20
        ),
        name="schur",
    )(present, absent, rows, high, low)


def swap_core(x):
    return lax.ppermute(x, "grp", [(i, i ^ 1) for i in range(8)])


def along_z(x, shift):
    return lax.ppermute(x, "grp", [(i, (i + 2 * shift) % 8) for i in range(8)])


def along_x(x, shift):
    return lax.ppermute(x, "col", [(i, (i + 4 * shift) % 16) for i in range(16)])


def along_y(x, shift):
    return lax.ppermute(x, "col", [(i, i // 4 * 4 + (i + shift) % 4) for i in range(16)])


def fetch(x, mover):
    return [x] + [mover(x, s) for s in (1, 2, 3)]


def plane_near(x):
    half = x.shape[0] // 2
    return jnp.stack(fetch(x[:half], along_y)), jnp.stack(fetch(x[half:], along_x))


def plane_far(near):
    return fetch(near[0], along_x) + fetch(near[1], along_y)


def pick(x, index, axis):
    return lax.dynamic_index_in_dim(x, index, axis, keepdims=False)


def join_cores(mine, other, core):
    lowest = jnp.where(core == 0, mine, other)
    highest = jnp.where(core == 0, other, mine)
    return jnp.concatenate([lowest, highest], axis=0)


def after(value, *others):
    return lax.optimization_barrier((value, *others))[0]


def program(pivot_blocks, coupling, block_map, parent_matrix):
    g = lax.axis_index("grp")
    c = lax.axis_index("col")
    pz, core = g // 2, g % 2
    px, py = c // 4, c % 4
    at_top = g == 0
    place = jnp.stack([g, c, pz, core, px, py]).astype(jnp.int32)

    gathered = lax.all_gather(coupling[0], "col", axis=0, tiled=True)

    lead_own = []
    for s in range(8):
        row, column = PANEL * (s % 2), BLK * (s // 2)
        piece = parent_matrix[row : row + PANEL, column : column + BLK]
        lead_own.append(lax.ppermute(piece, ("grp", "col"), [(0, s), (1, 8 + s)]))

    mapping = pick(block_map, g, 0)
    spots = jnp.arange(PBLK, dtype=jnp.int32)
    matches = mapping[None, :] == spots[:, None]
    position = jnp.sum(jnp.where(matches, jnp.arange(SBLK, dtype=jnp.int32)[None, :], 0), axis=1)
    present = jnp.any(matches, axis=1)
    rank = jnp.sum((spots[None, :] < spots[:, None]) & ~present[None, :], axis=1)
    slots = jnp.arange(SBLK, dtype=jnp.int32)
    absent = jnp.sum(
        jnp.where((rank[None, :] == slots[:, None]) & ~present[None, :], spots[None, :], 0), axis=1
    ).astype(jnp.int32)
    picks = jnp.arange(9, dtype=jnp.int32)
    spot = jnp.where(
        picks < 4, 4 * (c % 2) + picks, jnp.where(picks < 5, c // 2, 4 * c + picks - 5)
    )
    chosen = spot[:, None] == spots[None, :]
    where = jnp.sum(jnp.where(chosen, position[None, :], 0), axis=1)
    there = jnp.sum((chosen & present[None, :]).astype(jnp.int32), axis=1)

    pivot, mapping, where, there, absent, place = lax.optimization_barrier(
        (pivot_blocks[0], mapping, where, there, absent, place)
    )
    child_inv = child_factor(pivot)
    inv_high, inv_low, child_rows = child_rows_of(child_inv, coupling[0])
    gathered, child_rows = lax.optimization_barrier((gathered, child_rows))
    inverse = (inv_high, inv_low)

    piece = jax.ShapeDtypeStruct((PANEL, BLK), jnp.float32)
    lead_part = with_blocks(lead_part_kernel, 5, piece, where[:5], there[:5], inverse, gathered)
    for own in lead_own:
        lead_part = lead_part + own
    lead_halves = lead_part.reshape(2, PANEL // 2, BLK)
    lead_got = swap_core(pick(lead_halves, 1 - core, 0))
    wide = jax.ShapeDtypeStruct((PIV, PANEL), jnp.bfloat16)
    solved_high, solved_low = with_blocks(
        solved_kernel, 4, [wide, wide], where[5:], there[5:], inverse, gathered
    )
    lead_mine = pick(lead_halves, core, 0) + lead_got
    others = [along_z(lead_mine, s) for s in (1, 2, 3)]

    slab_all = schur_slab(mapping, absent, after(gathered, lead_got), solved_high, solved_low)
    update = lax.psum_scatter(slab_all, "grp", scatter_dimension=0, tiled=True)
    top_part = slab_all[:LEAD] + jnp.where(at_top, parent_matrix, 0.0)
    top_halves = top_part.reshape(2, PANEL, PANEL)

    lead_mine = lead_mine + others[0] + others[1] + others[2]
    lead_piece = join_cores(lead_mine, swap_core(lead_mine), core)
    top_got = swap_core(after(pick(top_halves, 1 - core, 0), lead_mine))
    lead_near = plane_near(lead_piece)
    lead_far = plane_far(lead_near)

    top_mine = (pick(top_halves, core, 0) + top_got).reshape(4, BLK, PANEL)
    top_mine = after(top_mine, lead_near)
    strips = [along_z(pick(top_mine, (pz + s) % 4, 0), s) for s in (1, 2, 3)]
    inv, low = lead_start(place[4:], lead_far, 2)
    strip = pick(top_mine, pz, 0) + strips[0] + strips[1] + strips[2]
    turn = [
        (gg * 16 + cc, (cc // 2) * 16 + 2 * gg + cc % 2) for gg in range(8) for cc in range(16)
    ]
    turned = lax.ppermute(strip, ("grp", "col"), turn)
    top_four = fetch(strip, along_z)
    inv, low = lead_next(inv, low, 2, 4)
    row_near = plane_near(turned)
    top_four = jnp.stack(top_four)
    other_four = swap_core(top_four)
    inv, low = lead_next(inv, low, 4, 6)
    row_far = plane_far(row_near)
    inv, low = lead_next(inv, low, 6, 8)

    change = solve(place, inv, low, top_four, other_four, row_far)

    below = (g > 0) & (c >= 2)
    keep_first = below | (at_top & (c > 0))
    keep_second = c >= 2
    assembled = after(parent_matrix, change) + update
    kept = jnp.where(jnp.arange(LEAD)[:, None] < PANEL, keep_first, keep_second)
    matrix = jnp.where(kept, assembled, 0.0) - change
    return (child_rows[None], matrix)


def solution(mesh):
    return jax.shard_map(
        program,
        mesh=mesh,
        in_specs=(P("grp", None, None), P("grp", "col", None), P(), P("grp", "col")),
        out_specs=(P("grp", "col", None), P("grp", "col")),
        check_vma=False,
    )
```

```python
import functools

import jax
import jax.numpy as jnp
from jax import lax
from jax.experimental import pallas as pl
from jax.experimental.pallas import tpu as pltpu
from jax.sharding import PartitionSpec as P


BLK = 128
PANEL = 512
LEAD = 1024
PIV = 1024
SBLK = 32
PBLK = 64

HIGHEST = lax.Precision.HIGHEST


def eliminate(work):
    order = BLK
    lane = lax.broadcasted_iota(jnp.int32, (8, order), 1)
    sub = lax.broadcasted_iota(jnp.int32, (8, order), 0)
    parts = order // 8
    rows = [work[8 * q : 8 * q + 8, :] for q in range(parts)]
    low = [jnp.zeros((8, order), jnp.float32) for _ in range(parts)]
    for q in range(parts):
        cols = [
            [
                jnp.broadcast_to(rows[p][:, 8 * q + k : 8 * q + k + 1], (8, order))
                for p in range(q, parts)
            ]
            for k in range(8)
        ]
        here = (lane >= 8 * q) & (lane < 8 * q + 8)
        mine = jnp.where(here, jnp.where(lane == sub + 8 * q, 1.0, 0.0), rows[q])
        fresh = []
        for k in range(8):
            root = lax.rsqrt(jnp.broadcast_to(cols[k][0][k : k + 1, :], (8, order)))
            cols[k] = [c * root for c in cols[k]]
            cols[k][0] = jnp.where(sub >= k, cols[k][0], 0.0)
            for m in range(k + 1, 8):
                scale = jnp.broadcast_to(cols[k][0][m : m + 1, :], (8, order))
                cols[m] = [a - b * scale for a, b in zip(cols[m], cols[k])]
            scaled = mine * root
            row = jnp.broadcast_to(scaled[k : k + 1, :], (8, order))
            fresh.append(row)
            mine = jnp.where(sub > k, mine - cols[k][0] * row, jnp.where(sub == k, scaled, mine))
        rows[q] = mine
        for p in range(q, parts):
            for k in range(8):
                low[p] = jnp.where(lane == 8 * q + k, cols[k][p - q], low[p])
        for p in range(q + 1, parts):
            acc = jnp.where(here, 0.0, rows[p])
            for k in range(8):
                acc = acc - cols[k][p - q] * fresh[k]
            rows[p] = acc
    for q in range(parts):
        rows[q] = jnp.where(lane <= sub + 8 * q, rows[q], 0.0)
    return jnp.concatenate(rows, axis=0), jnp.concatenate(low, axis=0)


def exact(a, b):
    return jnp.dot(a, b, precision=HIGHEST, preferred_element_type=jnp.float32)


def factor_steps(first, last, t_ref, l_ref, r_ref, terms=None):
    order = t_ref.shape[0]
    blocks = order // BLK

    def step(b, carry):
        at = pl.multiple_of(b * BLK, BLK)
        inv, low = eliminate(t_ref[pl.ds(at, BLK), pl.ds(at, BLK)])
        r_ref[...] = exact(inv, t_ref[pl.ds(at, BLK), :])
        r_ref[:, pl.ds(at, BLK)] = inv
        t_ref[pl.ds(at, BLK), :] = r_ref[...]
        if terms is not None:
            terms[0][...], terms[1][...] = split(r_ref[...])
        if l_ref is not None:
            l_ref[:, pl.ds(at, BLK)] = jnp.zeros((order, BLK), jnp.float32)
            l_ref[pl.ds(at, BLK), pl.ds(at, BLK)] = low

        def below(i, carry):
            to = pl.multiple_of(i * BLK, BLK)
            left = r_ref[:, pl.ds(to, BLK)].T
            if l_ref is not None:
                l_ref[pl.ds(to, BLK), pl.ds(at, BLK)] = left
            t_ref[pl.ds(to, BLK), pl.ds(at, BLK)] = jnp.zeros((BLK, BLK), jnp.float32)
            if terms is None:
                change = exact(left, r_ref[...])
            else:
                change = product(split(left), (terms[0][...], terms[1][...]))
            t_ref[pl.ds(to, BLK), :] = t_ref[pl.ds(to, BLK), :] - change
            return carry

        return lax.fori_loop(b + 1, blocks, below, carry)

    lax.fori_loop(first, last, step, 0)
    if last == blocks:
        for b in range(blocks - 1):
            width = order - BLK * (b + 1)
            t_ref[BLK * b : BLK * b + BLK, BLK * (b + 1) :] = jnp.zeros((BLK, width), jnp.float32)


def child_kernel(a_ref, t_ref, r_ref):
    t_ref[...] = a_ref[...]
    factor_steps(0, PIV // BLK, t_ref, None, r_ref)


def lead_start_kernel(last, place_ref, *refs):
    pieces, (t_ref, l_ref, r_ref, *terms) = refs[:8], refs[8:]
    core, px, py = place_ref[3], place_ref[4], place_ref[5]
    half = PANEL // 2
    for sx in range(4):
        for sy in range(4):
            x, y = (px + 4 - sx) % 4, (py + 4 - sy) % 4
            where = x * 4 + y
            row = (where % 2) * PANEL
            column = pl.multiple_of((where // 2) * BLK, BLK)
            first = pl.multiple_of(row + core * half, half)
            second = pl.multiple_of(row + (1 - core) * half, half)
            t_ref[pl.ds(first, half), pl.ds(column, BLK)] = pieces[sx][sy]
            t_ref[pl.ds(second, half), pl.ds(column, BLK)] = pieces[4 + sy][sx]
    factor_steps(0, last, t_ref, l_ref, r_ref, terms)


def lead_next_kernel(first, last, t_in, l_in, t_ref, l_ref, r_ref, *terms):
    factor_steps(first, last, t_ref, l_ref, r_ref, terms)


WHOLE = pl.BlockSpec(memory_space=pltpu.VMEM)
TABLE = pl.BlockSpec(memory_space=pltpu.SMEM)


def square(order):
    return jax.ShapeDtypeStruct((order, order), jnp.float32)


def limit(mib):
    return pltpu.CompilerParams(vmem_limit_bytes=mib << 20)


def work(gflop, mib):
    return pl.CostEstimate(
        flops=int(gflop * 10**9), bytes_accessed=mib << 20, transcendentals=0
    )


def child_factor(matrix):
    return pl.pallas_call(
        child_kernel,
        out_shape=square(PIV),
        in_specs=[WHOLE],
        out_specs=WHOLE,
        scratch_shapes=[pltpu.VMEM((BLK, PIV), jnp.float32)],
        cost_estimate=work(40, 12),
        compiler_params=limit(24),
        name="child_factor",
    )(matrix)


def lead_start(place, pieces, last):
    return pl.pallas_call(
        functools.partial(lead_start_kernel, last),
        out_shape=[square(LEAD)] * 2,
        in_specs=[TABLE] + [WHOLE] * 8,
        out_specs=[WHOLE] * 2,
        scratch_shapes=[pltpu.VMEM((BLK, LEAD), jnp.float32)]
        + [pltpu.VMEM((BLK, LEAD), jnp.bfloat16)] * 2,
        cost_estimate=work(10, 12),
        compiler_params=limit(24),
        name="lead_start",
    )(place, *pieces)


def lead_next(t, l, first, last):
    return pl.pallas_call(
        functools.partial(lead_next_kernel, first, last),
        out_shape=[square(LEAD)] * 2,
        in_specs=[WHOLE] * 2,
        out_specs=[WHOLE] * 2,
        input_output_aliases={0: 0, 1: 1},
        scratch_shapes=[pltpu.VMEM((BLK, LEAD), jnp.float32)]
        + [pltpu.VMEM((BLK, LEAD), jnp.bfloat16)] * 2,
        cost_estimate=work(10, 12),
        compiler_params=limit(24),
        name="lead_next",
    )(t, l)


def split(x):
    high = x.astype(jnp.bfloat16)
    return high, (x - high.astype(jnp.float32)).astype(jnp.bfloat16)


def product(a, b, turned=False):
    dims = (((1,), (1 if turned else 0,)), ((), ()))

    def one(x, y):
        return lax.dot_general(x, y, dims, preferred_element_type=jnp.float32)

    return one(a[0], b[0]) + one(a[0], b[1]) + one(a[1], b[0])


def rows_kernel(t_ref, c_ref, high_ref, low_ref, out_ref):
    high_ref[...], low_ref[...] = split(t_ref[...])
    out_ref[...] = product(split(c_ref[...]), (high_ref[...], low_ref[...]), True)


def child_rows_of(inverse, rows):
    half = jax.ShapeDtypeStruct((PIV, PIV), jnp.bfloat16)
    return pl.pallas_call(
        rows_kernel,
        out_shape=[half, half, jax.ShapeDtypeStruct(rows.shape, jnp.float32)],
        in_specs=[WHOLE] * 2,
        out_specs=[WHOLE] * 3,
        cost_estimate=work(2, 10),
        compiler_params=limit(32),
        name="child_rows",
    )(inverse, rows)


def load_blocks(count, where_ref, there_ref, rows_ref, got, sem):
    def copy(i):
        start = pl.multiple_of(where_ref[i] * BLK, BLK)
        return pltpu.make_async_copy(
            rows_ref.at[pl.ds(start, BLK)], got.at[pl.ds(i * BLK, BLK)], sem.at[i]
        )

    for i in range(count):
        copy(i).start()
    for i in range(count):
        copy(i).wait()

        @pl.when(there_ref[i] == 0)
        def _():
            got[i * BLK : i * BLK + BLK, :] = jnp.zeros((BLK, PIV), jnp.float32)


def lead_part_kernel(
    where_ref, there_ref, place_ref, high_ref, low_ref, own_ref, rows_ref, keep_ref, give_ref, got, sem
):
    load_blocks(5, where_ref, there_ref, rows_ref, got, sem)
    core = place_ref[3]
    half = PANEL // 2
    inverse = (high_ref[...], low_ref[...])
    half_way = product(split(got[4 * BLK :, :]), inverse, True)
    solved = product(split(half_way), inverse)
    part = product(split(got[: 4 * BLK, :]), split(solved), True)
    keep_ref[...] = own_ref[pl.ds(pl.multiple_of(core * half, half), half), :] - part[:half]
    give_ref[...] = own_ref[pl.ds(pl.multiple_of((1 - core) * half, half), half), :] - part[half:]


def top_kernel(
    where_ref, there_ref, spot_ref, place_ref, high_ref, low_ref, own_ref, rows_ref, keep_ref, give_ref, got, sem
):
    load_blocks(8, where_ref, there_ref, rows_ref, got, sem)
    solved = (high_ref[...], low_ref[...])
    at_top = place_ref[0] == 0
    for half, out_ref in ((0, keep_ref), (1, give_ref)):
        part = product(split(got[half * PANEL : half * PANEL + PANEL, :]), solved)
        for i in range(4):
            at = pl.multiple_of(spot_ref[half * 4 + i] * BLK, BLK)
            own = jnp.where(at_top, own_ref[pl.ds(at, BLK), :], 0.0)
            out_ref[i] = part[i * BLK : i * BLK + BLK] + own


def solved_kernel(where_ref, there_ref, high_ref, low_ref, rows_ref, oh_ref, ol_ref, got, sem):
    load_blocks(4, where_ref, there_ref, rows_ref, got, sem)
    inverse = (high_ref[...], low_ref[...])
    half_way = product(split(got[...]), inverse, True)
    solved = product(split(half_way), inverse)
    oh_ref[...], ol_ref[...] = split(-solved.T)


def with_blocks(kernel, count, out_shape, tables, inputs, rows):
    return pl.pallas_call(
        kernel,
        out_shape=out_shape,
        in_specs=[TABLE] * len(tables)
        + [WHOLE] * len(inputs)
        + [pl.BlockSpec(memory_space=pl.ANY)],
        out_specs=[WHOLE] * len(out_shape),
        scratch_shapes=[
            pltpu.VMEM((count * BLK, PIV), jnp.float32),
            pltpu.SemaphoreType.DMA((count,)),
        ],
        cost_estimate=work(3, 8),
        compiler_params=limit(40),
    )(*tables, *inputs, rows)


def solve_kernel(
    place_ref, t_ref, low_ref, mine_ref, other_ref, *refs
):
    pieces, (out_ref, th, tl, uh, ul, ph, pl_, fh, fl, xh, xl, rh, rl) = refs[:8], refs[8:]
    g, c, pz, core, px, py = [place_ref[i] for i in range(6)]
    half = PANEL

    th[...], tl[...] = split(t_ref[...])
    for i in range(4):
        for j in range(4):
            rows = slice(256 * j, 256 * j + 256)
            cols = slice(256 * i, 256 * i + 256)
            uh[rows, cols], ul[rows, cols] = split(t_ref[cols, rows].T)
    for s in range(4):
        z = (pz + 4 - s) % 4
        at = pl.multiple_of(core * half + z * BLK, BLK)
        ph[pl.ds(at, BLK), :], pl_[pl.ds(at, BLK), :] = split(mine_ref[s])
        at = pl.multiple_of((1 - core) * half + z * BLK, BLK)
        ph[pl.ds(at, BLK), :], pl_[pl.ds(at, BLK), :] = split(other_ref[s])

    def tiles(count, body):
        def one(i, carry):
            body(pl.ds(pl.multiple_of(i * 256, 256), 256))
            return carry

        lax.fori_loop(0, count, one, 0)

    for i in range(4):
        at, upto = slice(256 * i, 256 * i + 256), slice(0, 256 * i + 256)
        x = product((th[at, upto], tl[at, upto]), (ph[upto, :], pl_[upto, :]))
        fh[at, :], fl[at, :] = split(x)

    @pl.when(g == 0)
    def _():
        @pl.when(c == 0)
        def _():
            out_ref[...] = -low_ref[:, :half]

        @pl.when(c == 1)
        def _():
            out_ref[:half, :] = jnp.zeros((half, half), jnp.float32)
            out_ref[half:, :] = -low_ref[half:, half:]

        @pl.when(c >= 2)
        def _():
            out_ref[:half, :] = jnp.zeros((half, half), jnp.float32)
            left = split(low_ref[half:, :half])
            out_ref[half:, :] = product(left, (fh[:half, :], fl[:half, :]))

    @pl.when(g > 0)
    def _():
        @pl.when(c == 0)
        def _():
            xh[...], xl[...] = -uh[:, :half], -ul[:, :half]

        @pl.when(c == 1)
        def _():
            xh[...], xl[...] = -uh[:, half:], -ul[:, half:]

        @pl.when(c >= 2)
        def _():
            for i in range(4):
                at, since = slice(256 * i, 256 * i + 256), slice(256 * i, LEAD)
                x = product((uh[at, since], ul[at, since]), (fh[since, :], fl[since, :]))
                xh[at, :], xl[at, :] = split(x)

        for sx in range(4):
            for sy in range(4):
                x, y = (px + 4 - sx) % 4, (py + 4 - sy) % 4
                where = x * 4 + y
                source = where // 2
                row = pl.multiple_of((where % 2) * half, half)
                column = pl.multiple_of(((source % 2) * 4 + source // 2) * BLK, BLK)
                tile = jnp.concatenate([pieces[sx][sy], pieces[4 + sy][sx]], axis=0).T
                to = (pl.ds(row, half), pl.ds(column, BLK))
                rh[to], rl[to] = split(tile)

        def update(at):
            out_ref[at, :] = product((rh[at, :], rl[at, :]), (xh[...], xl[...]))

        tiles(4, update)


def solve(place, inverse, low, mine, other, pieces):
    def pair(rows, cols):
        return [pltpu.VMEM((rows, cols), jnp.bfloat16)] * 2

    return pl.pallas_call(
        solve_kernel,
        out_shape=jax.ShapeDtypeStruct((LEAD, PANEL), jnp.float32),
        in_specs=[TABLE] + [WHOLE] * 12,
        out_specs=WHOLE,
        scratch_shapes=pair(LEAD, LEAD) * 2 + pair(LEAD, PANEL) * 3 + pair(LEAD, LEAD),
        cost_estimate=work(10, 20),
        compiler_params=limit(36),
        name="solve",
    )(place, inverse, low, mine, other, *pieces)


def schur_kernel(step_blocks, present_ref, absent_ref, rows_ref, high_ref, low_ref, out_ref, buf, zero, sem, zsem):
    step = pl.program_id(0)
    steps = pl.num_programs(0)
    slot = lax.rem(step, 2)

    def put(which, index, to):
        return pltpu.make_async_copy(
            buf.at[which, pl.ds(index * BLK, BLK)],
            out_ref.at[pl.ds(pl.multiple_of(to * BLK, BLK), BLK)],
            sem.at[which, index],
        )

    def clear(index, to):
        return pltpu.make_async_copy(
            zero, out_ref.at[pl.ds(pl.multiple_of(to * BLK, BLK), BLK)], zsem.at[index]
        )

    @pl.when(step == 0)
    def _():
        zero[...] = jnp.zeros_like(zero)

    for i in range(step_blocks):
        clear(i, absent_ref[step * step_blocks + i]).start()
    x = rows_ref[...]
    xh = x.astype(jnp.bfloat16)
    xl = (x - xh.astype(jnp.float32)).astype(jnp.bfloat16)
    wh = high_ref[...]
    total = jnp.dot(xh, wh, preferred_element_type=jnp.float32)
    total += jnp.dot(xh, low_ref[...], preferred_element_type=jnp.float32)
    total += jnp.dot(xl, wh, preferred_element_type=jnp.float32)

    @pl.when(step >= 2)
    def _():
        for i in range(step_blocks):
            put(slot, i, 0).wait()

    buf[slot] = total
    for i in range(step_blocks):
        put(slot, i, present_ref[step * step_blocks + i]).start()
    for i in range(step_blocks):
        clear(i, 0).wait()

    @pl.when(step == steps - 1)
    def _():
        for i in range(step_blocks):
            put(slot, i, 0).wait()
            put(1 - slot, i, 0).wait()


def schur_slab(present, absent, rows, high, low, step_blocks=4):
    width = high.shape[1]
    steps = SBLK // step_blocks
    return pl.pallas_call(
        functools.partial(schur_kernel, step_blocks),
        out_shape=jax.ShapeDtypeStruct((PBLK * BLK, width), jnp.float32),
        grid_spec=pltpu.PrefetchScalarGridSpec(
            num_scalar_prefetch=2,
            grid=(steps,),
            in_specs=[
                pl.BlockSpec((step_blocks * BLK, PIV), lambda i, p, a: (i, 0)),
                pl.BlockSpec((PIV, width), lambda i, p, a: (0, 0)),
                pl.BlockSpec((PIV, width), lambda i, p, a: (0, 0)),
            ],
            out_specs=pl.BlockSpec(memory_space=pltpu.HBM),
            scratch_shapes=[
                pltpu.VMEM((2, step_blocks * BLK, width), jnp.float32),
                pltpu.VMEM((BLK, width), jnp.float32),
                pltpu.SemaphoreType.DMA((2, step_blocks)),
                pltpu.SemaphoreType.DMA((step_blocks,)),
            ],
        ),
        cost_estimate=pl.CostEstimate(
            flops=6 * SBLK * BLK * PIV * width, bytes_accessed=36 << 20, transcendentals=0
        ),
        compiler_params=pltpu.CompilerParams(
            dimension_semantics=("arbitrary",), vmem_limit_bytes=58 << 20
        ),
        name="schur",
    )(present, absent, rows, high, low)


def swap_core(x):
    return lax.ppermute(x, "grp", [(i, i ^ 1) for i in range(8)])


def along_z(x, shift):
    return lax.ppermute(x, "grp", [(i, (i + 2 * shift) % 8) for i in range(8)])


def along_x(x, shift):
    return lax.ppermute(x, "col", [(i, (i + 4 * shift) % 16) for i in range(16)])


def along_y(x, shift):
    return lax.ppermute(x, "col", [(i, i // 4 * 4 + (i + shift) % 4) for i in range(16)])


def fetch(x, mover):
    return [x] + [mover(x, s) for s in (1, 2, 3)]


def plane_near(x):
    half = x.shape[0] // 2
    return jnp.stack(fetch(x[:half], along_y)), jnp.stack(fetch(x[half:], along_x))


def plane_far(near):
    return fetch(near[0], along_x) + fetch(near[1], along_y)


def pick(x, index, axis):
    return lax.dynamic_index_in_dim(x, index, axis, keepdims=False)


def after(value, *others):
    return lax.optimization_barrier((value, *others))[0]


def program(pivot_blocks, coupling, block_map, parent_matrix):
    g = lax.axis_index("grp")
    c = lax.axis_index("col")
    pz, core = g // 2, g % 2
    px, py = c // 4, c % 4
    at_top = g == 0
    place = jnp.stack([g, c, pz, core, px, py]).astype(jnp.int32)

    gathered = lax.all_gather(coupling[0], "col", axis=0, tiled=True)

    lead_own = []
    for s in range(8):
        row, column = PANEL * (s % 2), BLK * (s // 2)
        piece = parent_matrix[row : row + PANEL, column : column + BLK]
        lead_own.append(lax.ppermute(piece, ("grp", "col"), [(0, s), (1, 8 + s)]))

    mapping = pick(block_map, g, 0)
    spots = jnp.arange(PBLK, dtype=jnp.int32)
    matches = mapping[None, :] == spots[:, None]
    position = jnp.sum(jnp.where(matches, jnp.arange(SBLK, dtype=jnp.int32)[None, :], 0), axis=1)
    present = jnp.any(matches, axis=1)
    rank = jnp.sum((spots[None, :] < spots[:, None]) & ~present[None, :], axis=1)
    slots = jnp.arange(SBLK, dtype=jnp.int32)
    absent = jnp.sum(
        jnp.where((rank[None, :] == slots[:, None]) & ~present[None, :], spots[None, :], 0), axis=1
    ).astype(jnp.int32)
    n = jnp.arange(17, dtype=jnp.int32)
    side = jnp.where(n % 4 < 2, core, 1 - core)
    lead_spot = 4 * (c % 2) + 2 * side + n % 2
    top_side = jnp.where(n < 13, core, 1 - core)
    top_spot = 4 * top_side + (pz + n - 9) % 4
    spot = jnp.where(
        n < 4, lead_spot, jnp.where(n < 5, c // 2, jnp.where(n < 9, 4 * c + n - 5, top_spot))
    ).astype(jnp.int32)
    chosen = spot[:, None] == spots[None, :]
    where = jnp.sum(jnp.where(chosen, position[None, :], 0), axis=1)
    there = jnp.sum((chosen & present[None, :]).astype(jnp.int32), axis=1)

    pivot, mapping, where, there, absent, place, spot = lax.optimization_barrier(
        (pivot_blocks[0], mapping, where, there, absent, place, spot)
    )
    child_inv = child_factor(pivot)
    inv_high, inv_low, child_rows = child_rows_of(child_inv, coupling[0])
    own = lead_own[0]
    for more in lead_own[1:]:
        own = own + more
    gathered, child_rows, own = lax.optimization_barrier((gathered, child_rows, own))

    half_piece = jax.ShapeDtypeStruct((PANEL // 2, BLK), jnp.float32)
    lead_keep, lead_give = with_blocks(
        lead_part_kernel,
        5,
        [half_piece] * 2,
        (where[:5], there[:5], place),
        (inv_high, inv_low, own),
        gathered,
    )
    lead_mine = lead_keep + swap_core(lead_give)
    others = [along_z(lead_mine, s) for s in (1, 2, 3)]
    wide = jax.ShapeDtypeStruct((PIV, PANEL), jnp.bfloat16)
    solved = with_blocks(
        solved_kernel, 4, [wide, wide], (where[5:9], there[5:9]), (inv_high, inv_low), gathered
    )
    lead_mine = lead_mine + others[0] + others[1] + others[2]
    lead_other = swap_core(lead_mine)

    half_top = jax.ShapeDtypeStruct((4, BLK, PANEL), jnp.float32)
    top_keep, top_give = with_blocks(
        top_kernel,
        8,
        [half_top] * 2,
        (where[9:], there[9:], spot[9:], place),
        (*solved, parent_matrix),
        gathered,
    )
    top_got = swap_core(top_give)
    lead_near = (
        jnp.stack(fetch(lead_mine, along_y)),
        jnp.stack(fetch(lead_other, along_x)),
    )
    lead_far = plane_far(lead_near)
    top_mine = after(top_keep + top_got, *lead_near)
    strips = [along_z(top_mine[s], s) for s in (1, 2, 3)]

    slab_all = schur_slab(mapping, absent, gathered, *solved)
    update = lax.psum_scatter(slab_all, "grp", scatter_dimension=0, tiled=True)

    strip = top_mine[0] + strips[0] + strips[1] + strips[2]
    turn = [
        (gg * 16 + cc, (cc // 2) * 16 + 2 * gg + cc % 2) for gg in range(8) for cc in range(16)
    ]
    turned = lax.ppermute(strip, ("grp", "col"), turn)
    top_four = fetch(strip, along_z)
    inv, low = lead_start(place, lead_far, 2)
    row_near = plane_near(turned)
    top_four = jnp.stack(top_four)
    other_four = swap_core(top_four)
    inv, low = lead_next(inv, low, 2, 4)
    row_far = plane_far(row_near)
    inv, low = lead_next(inv, low, 4, 8)

    change = solve(place, inv, low, top_four, other_four, row_far)

    below = (g > 0) & (c >= 2)
    keep_first = below | (at_top & (c > 0))
    keep_second = c >= 2
    assembled = after(parent_matrix, change) + update
    kept = jnp.where(jnp.arange(LEAD)[:, None] < PANEL, keep_first, keep_second)
    matrix = jnp.where(kept, assembled, 0.0) - change
    return (child_rows[None], matrix)


def solution(mesh):
    return jax.shard_map(
        program,
        mesh=mesh,
        in_specs=(P("grp", None, None), P("grp", "col", None), P(), P("grp", "col")),
        out_specs=(P("grp", "col", None), P("grp", "col")),
        check_vma=False,
    )
```

```python
import functools

import jax
import jax.numpy as jnp
from jax import lax
from jax.experimental import pallas as pl
from jax.experimental.pallas import tpu as pltpu
from jax.sharding import PartitionSpec as P


BLK = 128
PANEL = 512
LEAD = 1024
PIV = 1024
SBLK = 32
PBLK = 64

HIGHEST = lax.Precision.HIGHEST


def eliminate(work):
    order = BLK
    lane = lax.broadcasted_iota(jnp.int32, (8, order), 1)
    sub = lax.broadcasted_iota(jnp.int32, (8, order), 0)
    parts = order // 8
    rows = [work[8 * q : 8 * q + 8, :] for q in range(parts)]
    low = [jnp.zeros((8, order), jnp.float32) for _ in range(parts)]
    for q in range(parts):
        cols = [
            [
                jnp.broadcast_to(rows[p][:, 8 * q + k : 8 * q + k + 1], (8, order))
                for p in range(q, parts)
            ]
            for k in range(8)
        ]
        here = (lane >= 8 * q) & (lane < 8 * q + 8)
        mine = jnp.where(here, jnp.where(lane == sub + 8 * q, 1.0, 0.0), rows[q])
        fresh = []
        for k in range(8):
            raw = cols[k]
            root = lax.rsqrt(jnp.broadcast_to(raw[0][k : k + 1, :], (8, order)))
            scales = [jnp.broadcast_to(raw[0][m : m + 1, :], (8, order)) for m in range(k + 1, 8)]
            row = jnp.broadcast_to(mine[k : k + 1, :], (8, order)) * root
            fresh.append(row)
            done = [c * root for c in raw]
            for m in range(k + 1, 8):
                scale = scales[m - k - 1] * root
                cols[m] = [a - b * scale for a, b in zip(cols[m], done)]
            mine = jnp.where(sub > k, mine - done[0] * row, jnp.where(sub == k, row, mine))
            cols[k] = [jnp.where(sub >= k, done[0], 0.0)] + done[1:]
        rows[q] = mine
        for p in range(q, parts):
            for k in range(8):
                low[p] = jnp.where(lane == 8 * q + k, cols[k][p - q], low[p])
        for p in range(q + 1, parts):
            acc = jnp.where(here, 0.0, rows[p])
            for k in range(8):
                acc = acc - cols[k][p - q] * fresh[k]
            rows[p] = acc
    for q in range(parts):
        rows[q] = jnp.where(lane <= sub + 8 * q, rows[q], 0.0)
    return jnp.concatenate(rows, axis=0), jnp.concatenate(low, axis=0)


def exact(a, b):
    return jnp.dot(a, b, precision=HIGHEST, preferred_element_type=jnp.float32)


def factor_steps(first, last, t_ref, l_ref, r_ref, terms=None):
    order = t_ref.shape[0]
    blocks = order // BLK

    def step(b, carry):
        at = pl.multiple_of(b * BLK, BLK)
        inv, low = eliminate(t_ref[pl.ds(at, BLK), pl.ds(at, BLK)])
        r_ref[...] = exact(inv, t_ref[pl.ds(at, BLK), :])
        r_ref[:, pl.ds(at, BLK)] = inv
        t_ref[pl.ds(at, BLK), :] = r_ref[...]
        if terms is not None:
            terms[0][...], terms[1][...] = split(r_ref[...])
        if l_ref is not None:
            l_ref[:, pl.ds(at, BLK)] = jnp.zeros((order, BLK), jnp.float32)
            l_ref[pl.ds(at, BLK), pl.ds(at, BLK)] = low

        def below(i, carry):
            to = pl.multiple_of(i * BLK, BLK)
            left = r_ref[:, pl.ds(to, BLK)].T
            if l_ref is not None:
                l_ref[pl.ds(to, BLK), pl.ds(at, BLK)] = left
            t_ref[pl.ds(to, BLK), pl.ds(at, BLK)] = jnp.zeros((BLK, BLK), jnp.float32)
            if terms is None:
                change = exact(left, r_ref[...])
            else:
                change = product(split(left), (terms[0][...], terms[1][...]))
            t_ref[pl.ds(to, BLK), :] = t_ref[pl.ds(to, BLK), :] - change
            return carry

        return lax.fori_loop(b + 1, blocks, below, carry)

    lax.fori_loop(first, last, step, 0)
    if last == blocks:
        for b in range(blocks - 1):
            width = order - BLK * (b + 1)
            t_ref[BLK * b : BLK * b + BLK, BLK * (b + 1) :] = jnp.zeros((BLK, width), jnp.float32)


def child_kernel(a_ref, t_ref, r_ref):
    t_ref[...] = a_ref[...]
    factor_steps(0, PIV // BLK, t_ref, None, r_ref)


def lead_start_kernel(last, place_ref, *refs):
    pieces, (t_ref, l_ref, r_ref, *terms) = refs[:8], refs[8:]
    core, px, py = place_ref[3], place_ref[4], place_ref[5]
    half = PANEL // 2
    for sx in range(4):
        for sy in range(4):
            x, y = (px + 4 - sx) % 4, (py + 4 - sy) % 4
            where = x * 4 + y
            row = (where % 2) * PANEL
            column = pl.multiple_of((where // 2) * BLK, BLK)
            first = pl.multiple_of(row + core * half, half)
            second = pl.multiple_of(row + (1 - core) * half, half)
            t_ref[pl.ds(first, half), pl.ds(column, BLK)] = pieces[sx][sy]
            t_ref[pl.ds(second, half), pl.ds(column, BLK)] = pieces[4 + sy][sx]
    factor_steps(0, last, t_ref, l_ref, r_ref, terms)


def lead_next_kernel(first, last, t_in, l_in, t_ref, l_ref, r_ref, *terms):
    factor_steps(first, last, t_ref, l_ref, r_ref, terms)


WHOLE = pl.BlockSpec(memory_space=pltpu.VMEM)
TABLE = pl.BlockSpec(memory_space=pltpu.SMEM)


def square(order):
    return jax.ShapeDtypeStruct((order, order), jnp.float32)


def limit(mib):
    return pltpu.CompilerParams(vmem_limit_bytes=mib << 20)


def work(gflop, mib):
    return pl.CostEstimate(
        flops=int(gflop * 10**9), bytes_accessed=mib << 20, transcendentals=0
    )


def child_factor(matrix):
    return pl.pallas_call(
        child_kernel,
        out_shape=square(PIV),
        in_specs=[WHOLE],
        out_specs=WHOLE,
        scratch_shapes=[pltpu.VMEM((BLK, PIV), jnp.float32)],
        cost_estimate=work(40, 12),
        compiler_params=limit(24),
        name="child_factor",
    )(matrix)


def lead_start(place, pieces, last):
    return pl.pallas_call(
        functools.partial(lead_start_kernel, last),
        out_shape=[square(LEAD)] * 2,
        in_specs=[TABLE] + [WHOLE] * 8,
        out_specs=[WHOLE] * 2,
        scratch_shapes=[pltpu.VMEM((BLK, LEAD), jnp.float32)]
        + [pltpu.VMEM((BLK, LEAD), jnp.bfloat16)] * 2,
        cost_estimate=work(10, 12),
        compiler_params=limit(24),
        name="lead_start",
    )(place, *pieces)


def lead_next(t, l, first, last):
    return pl.pallas_call(
        functools.partial(lead_next_kernel, first, last),
        out_shape=[square(LEAD)] * 2,
        in_specs=[WHOLE] * 2,
        out_specs=[WHOLE] * 2,
        input_output_aliases={0: 0, 1: 1},
        scratch_shapes=[pltpu.VMEM((BLK, LEAD), jnp.float32)]
        + [pltpu.VMEM((BLK, LEAD), jnp.bfloat16)] * 2,
        cost_estimate=work(10, 12),
        compiler_params=limit(24),
        name="lead_next",
    )(t, l)


def split(x):
    high = x.astype(jnp.bfloat16)
    return high, (x - high.astype(jnp.float32)).astype(jnp.bfloat16)


def product(a, b, turned=False):
    dims = (((1,), (1 if turned else 0,)), ((), ()))

    def one(x, y):
        return lax.dot_general(x, y, dims, preferred_element_type=jnp.float32)

    return one(a[0], b[0]) + one(a[0], b[1]) + one(a[1], b[0])


def each(count, body, width=256):
    def one(i, carry):
        body(pl.ds(pl.multiple_of(i * width, width), width))
        return carry

    lax.fori_loop(0, count, one, 0)


def rows_kernel(t_ref, c_ref, high_ref, low_ref, out_ref, sh, sl):
    high_ref[...], low_ref[...] = split(t_ref[...])
    sh[...], sl[...] = split(c_ref[...])

    def body(at):
        inverse = (high_ref[at, :], low_ref[at, :])
        out_ref[:, at] = product((sh[...], sl[...]), inverse, True)

    each(PIV // 256, body)


def child_rows_of(inverse, rows):
    half = jax.ShapeDtypeStruct((PIV, PIV), jnp.bfloat16)
    return pl.pallas_call(
        rows_kernel,
        out_shape=[half, half, jax.ShapeDtypeStruct(rows.shape, jnp.float32)],
        in_specs=[WHOLE] * 2,
        out_specs=[WHOLE] * 3,
        scratch_shapes=[pltpu.VMEM(rows.shape, jnp.bfloat16)] * 2,
        cost_estimate=work(2, 10),
        compiler_params=limit(32),
        name="child_rows",
    )(inverse, rows)


def load_blocks(count, where_ref, there_ref, rows_ref, got, sem):
    def copy(i):
        start = pl.multiple_of(where_ref[i] * BLK, BLK)
        return pltpu.make_async_copy(
            rows_ref.at[pl.ds(start, BLK)], got.at[pl.ds(i * BLK, BLK)], sem.at[i]
        )

    for i in range(count):
        copy(i).start()
    for i in range(count):
        copy(i).wait()

        @pl.when(there_ref[i] == 0)
        def _():
            got[i * BLK : i * BLK + BLK, :] = jnp.zeros((BLK, PIV), jnp.float32)


def lead_part_kernel(
    where_ref, there_ref, place_ref, high_ref, low_ref, own_ref, rows_ref, keep_ref, give_ref, got, sem
):
    load_blocks(5, where_ref, there_ref, rows_ref, got, sem)
    core = place_ref[3]
    half = PANEL // 2
    inverse = (high_ref[...], low_ref[...])
    half_way = product(split(got[4 * BLK :, :]), inverse, True)
    solved = product(split(half_way), inverse)
    part = product(split(got[: 4 * BLK, :]), split(solved), True)
    keep_ref[...] = own_ref[pl.ds(pl.multiple_of(core * half, half), half), :] - part[:half]
    give_ref[...] = own_ref[pl.ds(pl.multiple_of((1 - core) * half, half), half), :] - part[half:]


def top_kernel(
    where_ref, there_ref, spot_ref, place_ref, high_ref, low_ref, own_ref, rows_ref, keep_ref, give_ref, got, sem
):
    load_blocks(8, where_ref, there_ref, rows_ref, got, sem)
    solved = (high_ref[...], low_ref[...])
    at_top = place_ref[0] == 0

    def one(i, carry):
        part = product(split(got[pl.ds(pl.multiple_of(i * 256, 256), 256), :]), solved)
        for j in range(2):
            at = pl.multiple_of(spot_ref[2 * i + j] * BLK, BLK)
            own = jnp.where(at_top, own_ref[pl.ds(at, BLK), :], 0.0)
            value = part[j * BLK : j * BLK + BLK] + own

            @pl.when(i < 2)
            def _():
                keep_ref[2 * i + j] = value

            @pl.when(i >= 2)
            def _():
                give_ref[2 * i + j - 4] = value

        return carry

    lax.fori_loop(0, 4, one, 0)


def solved_kernel(
    where_ref, there_ref, high_ref, low_ref, rows_ref, oh_ref, ol_ref, got, sem, sh, sl, yh, yl
):
    load_blocks(4, where_ref, there_ref, rows_ref, got, sem)
    sh[...], sl[...] = split(got[...])

    def half_way(at):
        inverse = (high_ref[at, :], low_ref[at, :])
        yh[:, at], yl[:, at] = split(product((sh[...], sl[...]), inverse, True))

    def solved(at):
        part = product((yh[...], yl[...]), (high_ref[:, at], low_ref[:, at]))
        oh_ref[at, :], ol_ref[at, :] = split(-part.T)

    each(PIV // 256, half_way)
    each(PIV // 256, solved)


def with_blocks(kernel, count, out_shape, tables, inputs, rows, scratch=()):
    return pl.pallas_call(
        kernel,
        out_shape=out_shape,
        in_specs=[TABLE] * len(tables)
        + [WHOLE] * len(inputs)
        + [pl.BlockSpec(memory_space=pl.ANY)],
        out_specs=[WHOLE] * len(out_shape),
        scratch_shapes=[
            pltpu.VMEM((count * BLK, PIV), jnp.float32),
            pltpu.SemaphoreType.DMA((count,)),
            *scratch,
        ],
        cost_estimate=work(3, 8),
        compiler_params=limit(40),
    )(*tables, *inputs, rows)


def solve_kernel(
    place_ref, t_ref, low_ref, top_ref, *refs
):
    pieces, (out_ref, th, tl, uh, ul, ph, pl_, fh, fl, xh, xl, rh, rl) = refs[:8], refs[8:]
    g, c, px, py = place_ref[0], place_ref[1], place_ref[4], place_ref[5]
    half = PANEL

    th[...], tl[...] = split(t_ref[...])
    for i in range(4):
        for j in range(4):
            rows = slice(256 * j, 256 * j + 256)
            cols = slice(256 * i, 256 * i + 256)
            uh[rows, cols], ul[rows, cols] = split(t_ref[cols, rows].T)
    for source in range(8):
        start = (source % 2 * 4 + source // 2) * BLK
        at = slice(start, start + BLK)
        ph[at, :], pl_[at, :] = split(top_ref[source])

    for i in range(4):
        at, upto = slice(256 * i, 256 * i + 256), slice(0, 256 * i + 256)
        x = product((th[at, upto], tl[at, upto]), (ph[upto, :], pl_[upto, :]))
        fh[at, :], fl[at, :] = split(x)

    @pl.when(g == 0)
    def _():
        @pl.when(c == 0)
        def _():
            out_ref[...] = -low_ref[:, :half]

        @pl.when(c == 1)
        def _():
            out_ref[:half, :] = jnp.zeros((half, half), jnp.float32)
            out_ref[half:, :] = -low_ref[half:, half:]

        @pl.when(c >= 2)
        def _():
            out_ref[:half, :] = jnp.zeros((half, half), jnp.float32)
            left = split(low_ref[half:, :half])
            out_ref[half:, :] = product(left, (fh[:half, :], fl[:half, :]))

    @pl.when(g > 0)
    def _():
        @pl.when(c == 0)
        def _():
            xh[...], xl[...] = -uh[:, :half], -ul[:, :half]

        @pl.when(c == 1)
        def _():
            xh[...], xl[...] = -uh[:, half:], -ul[:, half:]

        @pl.when(c >= 2)
        def _():
            for i in range(4):
                at, since = slice(256 * i, 256 * i + 256), slice(256 * i, LEAD)
                x = product((uh[at, since], ul[at, since]), (fh[since, :], fl[since, :]))
                xh[at, :], xl[at, :] = split(x)

        for sx in range(4):
            for sy in range(4):
                x, y = (px + 4 - sx) % 4, (py + 4 - sy) % 4
                where = x * 4 + y
                source = where // 2
                row = pl.multiple_of((where % 2) * half, half)
                column = pl.multiple_of(((source % 2) * 4 + source // 2) * BLK, BLK)
                tile = jnp.concatenate([pieces[sx][sy], pieces[4 + sy][sx]], axis=0).T
                to = (pl.ds(row, half), pl.ds(column, BLK))
                rh[to], rl[to] = split(tile)

        def update(at):
            out_ref[at, :] = product((rh[at, :], rl[at, :]), (xh[...], xl[...]))

        each(4, update)


def solve(place, inverse, low, top, pieces):
    def pair(rows, cols):
        return [pltpu.VMEM((rows, cols), jnp.bfloat16)] * 2

    return pl.pallas_call(
        solve_kernel,
        out_shape=jax.ShapeDtypeStruct((LEAD, PANEL), jnp.float32),
        in_specs=[TABLE] + [WHOLE] * 11,
        out_specs=WHOLE,
        scratch_shapes=pair(LEAD, LEAD) * 2 + pair(LEAD, PANEL) * 3 + pair(LEAD, LEAD),
        cost_estimate=work(10, 20),
        compiler_params=limit(36),
        name="solve",
    )(place, inverse, low, top, *pieces)


def schur_kernel(step_blocks, present_ref, absent_ref, rows_ref, high_ref, low_ref, out_ref, buf, zero, sem, zsem):
    step = pl.program_id(0)
    steps = pl.num_programs(0)
    slot = lax.rem(step, 2)

    def put(which, index, to):
        return pltpu.make_async_copy(
            buf.at[which, pl.ds(index * BLK, BLK)],
            out_ref.at[pl.ds(pl.multiple_of(to * BLK, BLK), BLK)],
            sem.at[which, index],
        )

    def clear(index, to):
        return pltpu.make_async_copy(
            zero, out_ref.at[pl.ds(pl.multiple_of(to * BLK, BLK), BLK)], zsem.at[index]
        )

    @pl.when(step == 0)
    def _():
        zero[...] = jnp.zeros_like(zero)

    for i in range(step_blocks):
        clear(i, absent_ref[step * step_blocks + i]).start()
    x = rows_ref[...]
    xh = x.astype(jnp.bfloat16)
    xl = (x - xh.astype(jnp.float32)).astype(jnp.bfloat16)
    wh = high_ref[...]
    total = jnp.dot(xh, wh, preferred_element_type=jnp.float32)
    total += jnp.dot(xh, low_ref[...], preferred_element_type=jnp.float32)
    total += jnp.dot(xl, wh, preferred_element_type=jnp.float32)

    @pl.when(step >= 2)
    def _():
        for i in range(step_blocks):
            put(slot, i, 0).wait()

    buf[slot] = total
    for i in range(step_blocks):
        put(slot, i, present_ref[step * step_blocks + i]).start()
    for i in range(step_blocks):
        clear(i, 0).wait()

    @pl.when(step == steps - 1)
    def _():
        for i in range(step_blocks):
            put(slot, i, 0).wait()
            put(1 - slot, i, 0).wait()


def schur_slab(present, absent, rows, high, low, step_blocks=4):
    width = high.shape[1]
    steps = SBLK // step_blocks
    return pl.pallas_call(
        functools.partial(schur_kernel, step_blocks),
        out_shape=jax.ShapeDtypeStruct((PBLK * BLK, width), jnp.float32),
        grid_spec=pltpu.PrefetchScalarGridSpec(
            num_scalar_prefetch=2,
            grid=(steps,),
            in_specs=[
                pl.BlockSpec((step_blocks * BLK, PIV), lambda i, p, a: (i, 0)),
                pl.BlockSpec((PIV, width), lambda i, p, a: (0, 0)),
                pl.BlockSpec((PIV, width), lambda i, p, a: (0, 0)),
            ],
            out_specs=pl.BlockSpec(memory_space=pltpu.HBM),
            scratch_shapes=[
                pltpu.VMEM((2, step_blocks * BLK, width), jnp.float32),
                pltpu.VMEM((BLK, width), jnp.float32),
                pltpu.SemaphoreType.DMA((2, step_blocks)),
                pltpu.SemaphoreType.DMA((step_blocks,)),
            ],
        ),
        cost_estimate=pl.CostEstimate(
            flops=6 * SBLK * BLK * PIV * width, bytes_accessed=36 << 20, transcendentals=0
        ),
        compiler_params=pltpu.CompilerParams(
            dimension_semantics=("arbitrary",), vmem_limit_bytes=58 << 20
        ),
        name="schur",
    )(present, absent, rows, high, low)


def swap_core(x):
    return lax.ppermute(x, "grp", [(i, i ^ 1) for i in range(8)])


def along_z(x, shift):
    return lax.ppermute(x, "grp", [(i, (i + 2 * shift) % 8) for i in range(8)])


def along_x(x, shift):
    return lax.ppermute(x, "col", [(i, (i + 4 * shift) % 16) for i in range(16)])


def along_y(x, shift):
    return lax.ppermute(x, "col", [(i, i // 4 * 4 + (i + shift) % 4) for i in range(16)])


def fetch(x, mover):
    return [x] + [mover(x, s) for s in (1, 2, 3)]


def plane_near(x):
    half = x.shape[0] // 2
    return jnp.stack(fetch(x[:half], along_y)), jnp.stack(fetch(x[half:], along_x))


def plane_far(near):
    return fetch(near[0], along_x) + fetch(near[1], along_y)


def pick(x, index, axis):
    return lax.dynamic_index_in_dim(x, index, axis, keepdims=False)


def after(value, *others):
    return lax.optimization_barrier((value, *others))[0]


def program(pivot_blocks, coupling, block_map, parent_matrix):
    g = lax.axis_index("grp")
    c = lax.axis_index("col")
    pz, core = g // 2, g % 2
    px, py = c // 4, c % 4
    at_top = g == 0
    place = jnp.stack([g, c, pz, core, px, py]).astype(jnp.int32)

    gathered = lax.all_gather(coupling[0], "col", axis=0, tiled=True)

    lead_own = []
    for s in range(8):
        row, column = PANEL * (s % 2), BLK * (s // 2)
        piece = parent_matrix[row : row + PANEL, column : column + BLK]
        lead_own.append(lax.ppermute(piece, ("grp", "col"), [(0, s), (1, 8 + s)]))

    mapping = pick(block_map, g, 0)
    spots = jnp.arange(PBLK, dtype=jnp.int32)
    matches = mapping[None, :] == spots[:, None]
    position = jnp.sum(jnp.where(matches, jnp.arange(SBLK, dtype=jnp.int32)[None, :], 0), axis=1)
    present = jnp.any(matches, axis=1)
    rank = jnp.sum((spots[None, :] < spots[:, None]) & ~present[None, :], axis=1)
    slots = jnp.arange(SBLK, dtype=jnp.int32)
    absent = jnp.sum(
        jnp.where((rank[None, :] == slots[:, None]) & ~present[None, :], spots[None, :], 0), axis=1
    ).astype(jnp.int32)
    n = jnp.arange(17, dtype=jnp.int32)
    side = jnp.where(n % 4 < 2, core, 1 - core)
    lead_spot = 4 * (c % 2) + 2 * side + n % 2
    top_side = jnp.where(n < 13, core, 1 - core)
    top_spot = 4 * top_side + (pz + n - 9) % 4
    spot = jnp.where(
        n < 4, lead_spot, jnp.where(n < 5, c // 2, jnp.where(n < 9, 4 * c + n - 5, top_spot))
    ).astype(jnp.int32)
    chosen = spot[:, None] == spots[None, :]
    where = jnp.sum(jnp.where(chosen, position[None, :], 0), axis=1)
    there = jnp.sum((chosen & present[None, :]).astype(jnp.int32), axis=1)

    pivot, mapping, where, there, absent, place, spot = lax.optimization_barrier(
        (pivot_blocks[0], mapping, where, there, absent, place, spot)
    )
    child_inv = child_factor(pivot)
    inv_high, inv_low, child_rows = child_rows_of(child_inv, coupling[0])
    own = lead_own[0]
    for more in lead_own[1:]:
        own = own + more
    gathered, child_rows, own = lax.optimization_barrier((gathered, child_rows, own))

    half_piece = jax.ShapeDtypeStruct((PANEL // 2, BLK), jnp.float32)
    lead_keep, lead_give = with_blocks(
        lead_part_kernel,
        5,
        [half_piece] * 2,
        (where[:5], there[:5], place),
        (inv_high, inv_low, own),
        gathered,
    )
    lead_got = swap_core(lead_give)
    wide = jax.ShapeDtypeStruct((PIV, PANEL), jnp.bfloat16)
    solved = with_blocks(
        solved_kernel,
        4,
        [wide, wide],
        (where[5:9], there[5:9]),
        (inv_high, inv_low),
        gathered,
        [pltpu.VMEM((PANEL, PIV), jnp.bfloat16)] * 4,
    )

    half_top = jax.ShapeDtypeStruct((4, BLK, PANEL), jnp.float32)
    top_keep, top_give = with_blocks(
        top_kernel,
        8,
        [half_top] * 2,
        (where[9:], there[9:], spot[9:], place),
        (*solved, parent_matrix),
        gathered,
    )
    top_got = swap_core(top_give)
    lead_mine = after(lead_keep + lead_got, top_give)
    others = [along_z(lead_mine, s) for s in (1, 2, 3)]
    top_mine = top_keep + top_got
    strips = [along_z(top_mine[s], s) for s in (1, 2, 3)]
    lead_mine = lead_mine + others[0] + others[1] + others[2]
    lead_other = swap_core(lead_mine)
    lead_near = (
        jnp.stack(fetch(lead_mine, along_y)),
        jnp.stack(fetch(lead_other, along_x)),
    )
    strip = top_mine[0] + strips[0] + strips[1] + strips[2]
    turn = [
        (gg * 16 + cc, (cc // 2) * 16 + 2 * gg + cc % 2) for gg in range(8) for cc in range(16)
    ]
    turned = lax.ppermute(strip, ("grp", "col"), turn)
    top_all = lax.all_gather(strip, "grp", axis=0)

    slab_all = schur_slab(mapping, absent, after(gathered, strip), *solved)
    update = lax.psum_scatter(slab_all, "grp", scatter_dimension=0, tiled=True)

    near_a, near_b, _, top_all = lax.optimization_barrier((*lead_near, slab_all, top_all))
    lead_far = plane_far((near_a, near_b))
    row_near = plane_near(turned)
    inv, low = lead_start(place, lead_far, 4)
    row_far = plane_far(row_near)
    inv, low = lead_next(inv, low, 4, 8)

    change = solve(place, inv, low, top_all, row_far)

    below = (g > 0) & (c >= 2)
    keep_first = below | (at_top & (c > 0))
    keep_second = c >= 2
    kept = jnp.where(jnp.arange(LEAD)[:, None] < PANEL, keep_first, keep_second)
    base = jnp.where(kept, parent_matrix, 0.0) - change
    matrix = lax.optimization_barrier(base) + jnp.where(kept, update, 0.0)
    return (child_rows[None], matrix)


def solution(mesh):
    return jax.shard_map(
        program,
        mesh=mesh,
        in_specs=(P("grp", None, None), P("grp", "col", None), P(), P("grp", "col")),
        out_specs=(P("grp", "col", None), P("grp", "col")),
        check_vma=False,
    )
```

```python
import functools

import jax
import jax.numpy as jnp
from jax import lax
from jax.experimental import pallas as pl
from jax.experimental.pallas import tpu as pltpu
from jax.sharding import PartitionSpec as P


BLK = 128
PANEL = 512
LEAD = 1024
PIV = 1024
SBLK = 32
PBLK = 64

HIGHEST = lax.Precision.HIGHEST


def eliminate(work):
    order = BLK
    lane = lax.broadcasted_iota(jnp.int32, (8, order), 1)
    sub = lax.broadcasted_iota(jnp.int32, (8, order), 0)
    parts = order // 8
    rows = [work[8 * q : 8 * q + 8, :] for q in range(parts)]
    low = [jnp.zeros((8, order), jnp.float32) for _ in range(parts)]
    for q in range(parts):
        cols = [
            [
                jnp.broadcast_to(rows[p][:, 8 * q + k : 8 * q + k + 1], (8, order))
                for p in range(q, parts)
            ]
            for k in range(8)
        ]
        here = (lane >= 8 * q) & (lane < 8 * q + 8)
        mine = jnp.where(here, jnp.where(lane == sub + 8 * q, 1.0, 0.0), rows[q])
        fresh = []
        for k in range(8):
            raw = cols[k]
            root = lax.rsqrt(jnp.broadcast_to(raw[0][k : k + 1, :], (8, order)))
            scales = [jnp.broadcast_to(raw[0][m : m + 1, :], (8, order)) for m in range(k + 1, 8)]
            row = jnp.broadcast_to(mine[k : k + 1, :], (8, order)) * root
            fresh.append(row)
            done = [c * root for c in raw]
            for m in range(k + 1, 8):
                scale = scales[m - k - 1] * root
                cols[m] = [a - b * scale for a, b in zip(cols[m], done)]
            mine = jnp.where(sub > k, mine - done[0] * row, jnp.where(sub == k, row, mine))
            cols[k] = [jnp.where(sub >= k, done[0], 0.0)] + done[1:]
        rows[q] = mine
        for p in range(q, parts):
            for k in range(8):
                low[p] = jnp.where(lane == 8 * q + k, cols[k][p - q], low[p])
        for p in range(q + 1, parts):
            acc = jnp.where(here, 0.0, rows[p])
            for k in range(8):
                acc = acc - cols[k][p - q] * fresh[k]
            rows[p] = acc
    for q in range(parts):
        rows[q] = jnp.where(lane <= sub + 8 * q, rows[q], 0.0)
    return jnp.concatenate(rows, axis=0), jnp.concatenate(low, axis=0)


def exact(a, b):
    return jnp.dot(a, b, precision=HIGHEST, preferred_element_type=jnp.float32)


def factor_steps(first, last, t_ref, l_ref, r_ref, terms=None):
    order = t_ref.shape[0]
    blocks = order // BLK

    def keep(rows):
        if terms is not None:
            terms[0][rows, :], terms[1][rows, :] = split(r_ref[rows, :])

    def change(left, rows):
        if terms is None:
            return exact(left, r_ref[rows, :])
        return product(split(left), (terms[0][rows, :], terms[1][rows, :]))

    def pair(p, carry):
        base = pl.multiple_of(p * 2 * BLK, 2 * BLK)
        out = pl.multiple_of(base - first * BLK, 2 * BLK)
        if l_ref is not None:
            l_ref[:, pl.ds(out, 2 * BLK)] = jnp.zeros((order, 2 * BLK), jnp.float32)

        def one(j, carry):
            at = pl.multiple_of(base + j * BLK, BLK)
            rows = pl.ds(pl.multiple_of(j * BLK, BLK), BLK)
            inv, low = eliminate(t_ref[pl.ds(at, BLK), pl.ds(at, BLK)])
            r_ref[rows, :] = exact(inv, t_ref[pl.ds(at, BLK), :])
            r_ref[rows, pl.ds(at, BLK)] = inv
            t_ref[pl.ds(at, BLK), :] = r_ref[rows, :]
            if l_ref is not None:
                to = pl.multiple_of(out + j * BLK, BLK)
                l_ref[pl.ds(at, BLK), pl.ds(to, BLK)] = low
            keep(rows)

            @pl.when(j == 0)
            def _():
                to = pl.multiple_of(base + BLK, BLK)
                top = slice(0, BLK)
                left = r_ref[top, pl.ds(to, BLK)].T
                if l_ref is not None:
                    l_ref[pl.ds(to, BLK), pl.ds(out, BLK)] = left
                t_ref[pl.ds(to, BLK), pl.ds(base, BLK)] = jnp.zeros((BLK, BLK), jnp.float32)
                t_ref[pl.ds(to, BLK), :] = t_ref[pl.ds(to, BLK), :] - change(left, top)
                r_ref[top, pl.ds(to, BLK)] = jnp.zeros((BLK, BLK), jnp.float32)
                keep(top)

            return carry

        lax.fori_loop(0, 2, one, 0)

        def below(i, carry):
            to = pl.multiple_of(i * BLK, BLK)
            left = r_ref[:, pl.ds(to, BLK)].T
            if l_ref is not None:
                l_ref[pl.ds(to, BLK), pl.ds(out, 2 * BLK)] = left
            t_ref[pl.ds(to, BLK), pl.ds(base, 2 * BLK)] = jnp.zeros((BLK, 2 * BLK), jnp.float32)
            t_ref[pl.ds(to, BLK), :] = t_ref[pl.ds(to, BLK), :] - change(left, slice(0, 2 * BLK))
            return carry

        return lax.fori_loop(2 * p + 2, blocks, below, carry)

    lax.fori_loop(first // 2, last // 2, pair, 0)
    if last == blocks:
        for b in range(blocks - 1):
            width = order - BLK * (b + 1)
            t_ref[BLK * b : BLK * b + BLK, BLK * (b + 1) :] = jnp.zeros((BLK, width), jnp.float32)


def child_kernel(a_ref, t_ref, r_ref):
    t_ref[...] = a_ref[...]
    factor_steps(0, PIV // BLK, t_ref, None, r_ref)


def lead_start_kernel(last, place_ref, *refs):
    pieces, (t_ref, l_ref, r_ref, *terms) = refs[:8], refs[8:]
    core, px, py = place_ref[3], place_ref[4], place_ref[5]
    half = PANEL // 2
    for sx in range(4):
        for sy in range(4):
            x, y = (px + 4 - sx) % 4, (py + 4 - sy) % 4
            where = x * 4 + y
            row = (where % 2) * PANEL
            column = pl.multiple_of((where // 2) * BLK, BLK)
            first = pl.multiple_of(row + core * half, half)
            second = pl.multiple_of(row + (1 - core) * half, half)
            t_ref[pl.ds(first, half), pl.ds(column, BLK)] = pieces[sx][sy]
            t_ref[pl.ds(second, half), pl.ds(column, BLK)] = pieces[4 + sy][sx]
    factor_steps(0, last, t_ref, l_ref, r_ref, terms)


def lead_next_kernel(first, last, t_in, t_ref, l_ref, r_ref, *terms):
    t_ref[...] = t_in[...]
    factor_steps(first, last, t_ref, l_ref, r_ref, terms)


WHOLE = pl.BlockSpec(memory_space=pltpu.VMEM)
TABLE = pl.BlockSpec(memory_space=pltpu.SMEM)


def square(order):
    return jax.ShapeDtypeStruct((order, order), jnp.float32)


def limit(mib):
    return pltpu.CompilerParams(vmem_limit_bytes=mib << 20)


def work(gflop, mib):
    return pl.CostEstimate(
        flops=int(gflop * 10**9), bytes_accessed=mib << 20, transcendentals=0
    )


def child_factor(matrix):
    return pl.pallas_call(
        child_kernel,
        out_shape=square(PIV),
        in_specs=[WHOLE],
        out_specs=WHOLE,
        scratch_shapes=[pltpu.VMEM((2 * BLK, PIV), jnp.float32)],
        cost_estimate=work(40, 12),
        compiler_params=limit(24),
        name="child_factor",
    )(matrix)


def lead_call(kernel, columns, in_specs):
    return pl.pallas_call(
        kernel,
        out_shape=[square(LEAD), jax.ShapeDtypeStruct((LEAD, columns), jnp.float32)],
        in_specs=in_specs,
        out_specs=[WHOLE] * 2,
        scratch_shapes=[pltpu.VMEM((2 * BLK, LEAD), jnp.float32)]
        + [pltpu.VMEM((2 * BLK, LEAD), jnp.bfloat16)] * 2,
        cost_estimate=work(10, 12),
        compiler_params=limit(24),
    )


def lead_start(place, pieces, last):
    kernel = functools.partial(lead_start_kernel, last)
    return lead_call(kernel, last * BLK, [TABLE] + [WHOLE] * 8)(place, *pieces)


def lead_next(t, first, last):
    kernel = functools.partial(lead_next_kernel, first, last)
    return lead_call(kernel, (last - first) * BLK, [WHOLE])(t)


def split(x):
    high = x.astype(jnp.bfloat16)
    return high, (x - high.astype(jnp.float32)).astype(jnp.bfloat16)


def product(a, b, turned=False):
    dims = (((1,), (1 if turned else 0,)), ((), ()))

    def one(x, y):
        return lax.dot_general(x, y, dims, preferred_element_type=jnp.float32)

    return one(a[0], b[0]) + one(a[0], b[1]) + one(a[1], b[0])


def each(count, body, width=256):
    def one(i, carry):
        body(pl.ds(pl.multiple_of(i * width, width), width))
        return carry

    lax.fori_loop(0, count, one, 0)


def rows_kernel(t_ref, c_ref, high_ref, low_ref, out_ref, sh, sl):
    high_ref[...], low_ref[...] = split(t_ref[...])
    sh[...], sl[...] = split(c_ref[...])

    def body(at):
        inverse = (high_ref[at, :], low_ref[at, :])
        out_ref[:, at] = product((sh[...], sl[...]), inverse, True)

    each(PIV // 256, body)


def child_rows_of(inverse, rows):
    half = jax.ShapeDtypeStruct((PIV, PIV), jnp.bfloat16)
    return pl.pallas_call(
        rows_kernel,
        out_shape=[half, half, jax.ShapeDtypeStruct(rows.shape, jnp.float32)],
        in_specs=[WHOLE] * 2,
        out_specs=[WHOLE] * 3,
        scratch_shapes=[pltpu.VMEM(rows.shape, jnp.bfloat16)] * 2,
        cost_estimate=work(2, 10),
        compiler_params=limit(32),
        name="child_rows",
    )(inverse, rows)


def load_blocks(count, where_ref, there_ref, rows_ref, got, sem):
    def copy(i):
        start = pl.multiple_of(where_ref[i] * BLK, BLK)
        return pltpu.make_async_copy(
            rows_ref.at[pl.ds(start, BLK)], got.at[pl.ds(i * BLK, BLK)], sem.at[i]
        )

    for i in range(count):
        copy(i).start()
    for i in range(count):
        copy(i).wait()

        @pl.when(there_ref[i] == 0)
        def _():
            got[i * BLK : i * BLK + BLK, :] = jnp.zeros((BLK, PIV), jnp.float32)


def lead_part_kernel(
    where_ref, there_ref, place_ref, high_ref, low_ref, own_ref, rows_ref, keep_ref, give_ref, got, sem
):
    load_blocks(5, where_ref, there_ref, rows_ref, got, sem)
    core = place_ref[3]
    half = PANEL // 2
    inverse = (high_ref[...], low_ref[...])
    half_way = product(split(got[4 * BLK :, :]), inverse, True)
    solved = product(split(half_way), inverse)
    part = product(split(got[: 4 * BLK, :]), split(solved), True)
    keep_ref[...] = own_ref[pl.ds(pl.multiple_of(core * half, half), half), :] - part[:half]
    give_ref[...] = own_ref[pl.ds(pl.multiple_of((1 - core) * half, half), half), :] - part[half:]


def top_kernel(
    where_ref, there_ref, spot_ref, place_ref, high_ref, low_ref, own_ref, rows_ref, keep_ref, give_ref, got, sem
):
    load_blocks(8, where_ref, there_ref, rows_ref, got, sem)
    solved = (high_ref[...], low_ref[...])
    at_top = place_ref[0] == 0
    for half, out_ref in ((0, keep_ref), (1, give_ref)):
        part = product(split(got[half * PANEL : half * PANEL + PANEL, :]), solved)
        for i in range(4):
            at = pl.multiple_of(spot_ref[half * 4 + i] * BLK, BLK)
            own = jnp.where(at_top, own_ref[pl.ds(at, BLK), :], 0.0)
            out_ref[i] = part[i * BLK : i * BLK + BLK] + own


def solved_kernel(where_ref, there_ref, high_ref, low_ref, rows_ref, oh_ref, ol_ref, got, sem):
    load_blocks(4, where_ref, there_ref, rows_ref, got, sem)
    inverse = (high_ref[...], low_ref[...])
    half_way = product(split(got[...]), inverse, True)
    solved = product(split(half_way), inverse)
    oh_ref[...], ol_ref[...] = split(-solved.T)


def with_blocks(kernel, count, out_shape, tables, inputs, rows):
    return pl.pallas_call(
        kernel,
        out_shape=out_shape,
        in_specs=[TABLE] * len(tables)
        + [WHOLE] * len(inputs)
        + [pl.BlockSpec(memory_space=pl.ANY)],
        out_specs=[WHOLE] * len(out_shape),
        scratch_shapes=[
            pltpu.VMEM((count * BLK, PIV), jnp.float32),
            pltpu.SemaphoreType.DMA((count,)),
        ],
        cost_estimate=work(3, 8),
        compiler_params=limit(40),
    )(*tables, *inputs, rows)


def solve_kernel(
    place_ref, t_ref, first_ref, second_ref, top_ref, *refs
):
    pieces, (out_ref, th, tl, uh, ul, ph, pl_, fh, fl, xh, xl, rh, rl) = refs[:8], refs[8:]
    g, c, px, py = place_ref[0], place_ref[1], place_ref[4], place_ref[5]
    half = PANEL

    th[...], tl[...] = split(t_ref[...])
    for i in range(4):
        for j in range(4):
            rows = slice(256 * j, 256 * j + 256)
            cols = slice(256 * i, 256 * i + 256)
            uh[rows, cols], ul[rows, cols] = split(t_ref[cols, rows].T)
    for source in range(8):
        start = (source % 2 * 4 + source // 2) * BLK
        at = slice(start, start + BLK)
        ph[at, :], pl_[at, :] = split(top_ref[source])

    for i in range(4):
        at, upto = slice(256 * i, 256 * i + 256), slice(0, 256 * i + 256)
        x = product((th[at, upto], tl[at, upto]), (ph[upto, :], pl_[upto, :]))
        fh[at, :], fl[at, :] = split(x)

    @pl.when(g == 0)
    def _():
        @pl.when(c == 0)
        def _():
            out_ref[...] = -first_ref[...]

        @pl.when(c == 1)
        def _():
            out_ref[:half, :] = jnp.zeros((half, half), jnp.float32)
            out_ref[half:, :] = -second_ref[half:, :]

        @pl.when(c >= 2)
        def _():
            out_ref[:half, :] = jnp.zeros((half, half), jnp.float32)
            left = split(first_ref[half:, :])
            out_ref[half:, :] = product(left, (fh[:half, :], fl[:half, :]))

    @pl.when(g > 0)
    def _():
        @pl.when(c == 0)
        def _():
            xh[...], xl[...] = -uh[:, :half], -ul[:, :half]

        @pl.when(c == 1)
        def _():
            xh[...], xl[...] = -uh[:, half:], -ul[:, half:]

        @pl.when(c >= 2)
        def _():
            for i in range(4):
                at, since = slice(256 * i, 256 * i + 256), slice(256 * i, LEAD)
                x = product((uh[at, since], ul[at, since]), (fh[since, :], fl[since, :]))
                xh[at, :], xl[at, :] = split(x)

        for sx in range(4):
            for sy in range(4):
                x, y = (px + 4 - sx) % 4, (py + 4 - sy) % 4
                where = x * 4 + y
                source = where // 2
                row = pl.multiple_of((where % 2) * half, half)
                column = pl.multiple_of(((source % 2) * 4 + source // 2) * BLK, BLK)
                tile = jnp.concatenate([pieces[sx][sy], pieces[4 + sy][sx]], axis=0).T
                to = (pl.ds(row, half), pl.ds(column, BLK))
                rh[to], rl[to] = split(tile)

        def update(at):
            out_ref[at, :] = product((rh[at, :], rl[at, :]), (xh[...], xl[...]))

        each(4, update)


def solve(place, inverse, first, second, top, pieces):
    def pair(rows, cols):
        return [pltpu.VMEM((rows, cols), jnp.bfloat16)] * 2

    return pl.pallas_call(
        solve_kernel,
        out_shape=jax.ShapeDtypeStruct((LEAD, PANEL), jnp.float32),
        in_specs=[TABLE] + [WHOLE] * 12,
        out_specs=WHOLE,
        scratch_shapes=pair(LEAD, LEAD) * 2 + pair(LEAD, PANEL) * 3 + pair(LEAD, LEAD),
        cost_estimate=work(10, 20),
        compiler_params=limit(36),
        name="solve",
    )(place, inverse, first, second, top, *pieces)


def schur_kernel(step_blocks, present_ref, absent_ref, rows_ref, high_ref, low_ref, out_ref, buf, zero, sem, zsem):
    step = pl.program_id(0)
    steps = pl.num_programs(0)
    slot = lax.rem(step, 2)

    def put(which, index, to):
        return pltpu.make_async_copy(
            buf.at[which, pl.ds(index * BLK, BLK)],
            out_ref.at[pl.ds(pl.multiple_of(to * BLK, BLK), BLK)],
            sem.at[which, index],
        )

    def clear(index, to):
        return pltpu.make_async_copy(
            zero, out_ref.at[pl.ds(pl.multiple_of(to * BLK, BLK), BLK)], zsem.at[index]
        )

    @pl.when(step == 0)
    def _():
        zero[...] = jnp.zeros_like(zero)

    for i in range(step_blocks):
        clear(i, absent_ref[step * step_blocks + i]).start()
    x = rows_ref[...]
    xh = x.astype(jnp.bfloat16)
    xl = (x - xh.astype(jnp.float32)).astype(jnp.bfloat16)
    wh = high_ref[...]
    total = jnp.dot(xh, wh, preferred_element_type=jnp.float32)
    total += jnp.dot(xh, low_ref[...], preferred_element_type=jnp.float32)
    total += jnp.dot(xl, wh, preferred_element_type=jnp.float32)

    @pl.when(step >= 2)
    def _():
        for i in range(step_blocks):
            put(slot, i, 0).wait()

    buf[slot] = total
    for i in range(step_blocks):
        put(slot, i, present_ref[step * step_blocks + i]).start()
    for i in range(step_blocks):
        clear(i, 0).wait()

    @pl.when(step == steps - 1)
    def _():
        for i in range(step_blocks):
            put(slot, i, 0).wait()
            put(1 - slot, i, 0).wait()


def schur_slab(present, absent, rows, high, low, step_blocks=4):
    width = high.shape[1]
    steps = SBLK // step_blocks
    return pl.pallas_call(
        functools.partial(schur_kernel, step_blocks),
        out_shape=jax.ShapeDtypeStruct((PBLK * BLK, width), jnp.float32),
        grid_spec=pltpu.PrefetchScalarGridSpec(
            num_scalar_prefetch=2,
            grid=(steps,),
            in_specs=[
                pl.BlockSpec((step_blocks * BLK, PIV), lambda i, p, a: (i, 0)),
                pl.BlockSpec((PIV, width), lambda i, p, a: (0, 0)),
                pl.BlockSpec((PIV, width), lambda i, p, a: (0, 0)),
            ],
            out_specs=pl.BlockSpec(memory_space=pltpu.HBM),
            scratch_shapes=[
                pltpu.VMEM((2, step_blocks * BLK, width), jnp.float32),
                pltpu.VMEM((BLK, width), jnp.float32),
                pltpu.SemaphoreType.DMA((2, step_blocks)),
                pltpu.SemaphoreType.DMA((step_blocks,)),
            ],
        ),
        cost_estimate=pl.CostEstimate(
            flops=6 * SBLK * BLK * PIV * width, bytes_accessed=36 << 20, transcendentals=0
        ),
        compiler_params=pltpu.CompilerParams(
            dimension_semantics=("arbitrary",), vmem_limit_bytes=58 << 20
        ),
        name="schur",
    )(present, absent, rows, high, low)


def swap_core(x):
    return lax.ppermute(x, "grp", [(i, i ^ 1) for i in range(8)])


def along_z(x, shift):
    return lax.ppermute(x, "grp", [(i, (i + 2 * shift) % 8) for i in range(8)])


def along_x(x, shift):
    return lax.ppermute(x, "col", [(i, (i + 4 * shift) % 16) for i in range(16)])


def along_y(x, shift):
    return lax.ppermute(x, "col", [(i, i // 4 * 4 + (i + shift) % 4) for i in range(16)])


def fetch(x, mover):
    return [x] + [mover(x, s) for s in (1, 2, 3)]


def plane_near(x):
    half = x.shape[0] // 2
    return jnp.stack(fetch(x[:half], along_y)), jnp.stack(fetch(x[half:], along_x))


def plane_far(near):
    return fetch(near[0], along_x) + fetch(near[1], along_y)


def pick(x, index, axis):
    return lax.dynamic_index_in_dim(x, index, axis, keepdims=False)


def after(value, *others):
    return lax.optimization_barrier((value, *others))[0]


def program(pivot_blocks, coupling, block_map, parent_matrix):
    g = lax.axis_index("grp")
    c = lax.axis_index("col")
    pz, core = g // 2, g % 2
    px, py = c // 4, c % 4
    at_top = g == 0
    place = jnp.stack([g, c, pz, core, px, py]).astype(jnp.int32)

    gathered = lax.all_gather(coupling[0], "col", axis=0, tiled=True)

    lead_own = []
    for s in range(8):
        row, column = PANEL * (s % 2), BLK * (s // 2)
        piece = parent_matrix[row : row + PANEL, column : column + BLK]
        lead_own.append(lax.ppermute(piece, ("grp", "col"), [(0, s), (1, 8 + s)]))

    mapping = pick(block_map, g, 0)
    spots = jnp.arange(PBLK, dtype=jnp.int32)
    matches = mapping[None, :] == spots[:, None]
    position = jnp.sum(jnp.where(matches, jnp.arange(SBLK, dtype=jnp.int32)[None, :], 0), axis=1)
    present = jnp.any(matches, axis=1)
    rank = jnp.sum((spots[None, :] < spots[:, None]) & ~present[None, :], axis=1)
    slots = jnp.arange(SBLK, dtype=jnp.int32)
    absent = jnp.sum(
        jnp.where((rank[None, :] == slots[:, None]) & ~present[None, :], spots[None, :], 0), axis=1
    ).astype(jnp.int32)
    n = jnp.arange(17, dtype=jnp.int32)
    side = jnp.where(n % 4 < 2, core, 1 - core)
    lead_spot = 4 * (c % 2) + 2 * side + n % 2
    top_side = jnp.where(n < 13, core, 1 - core)
    top_spot = 4 * top_side + (pz + n - 9) % 4
    spot = jnp.where(
        n < 4, lead_spot, jnp.where(n < 5, c // 2, jnp.where(n < 9, 4 * c + n - 5, top_spot))
    ).astype(jnp.int32)
    chosen = spot[:, None] == spots[None, :]
    where = jnp.sum(jnp.where(chosen, position[None, :], 0), axis=1)
    there = jnp.sum((chosen & present[None, :]).astype(jnp.int32), axis=1)

    pivot, mapping, where, there, absent, place, spot = lax.optimization_barrier(
        (pivot_blocks[0], mapping, where, there, absent, place, spot)
    )
    child_inv = child_factor(pivot)
    inv_high, inv_low, child_rows = child_rows_of(child_inv, coupling[0])
    own = lead_own[0]
    for more in lead_own[1:]:
        own = own + more
    gathered, child_rows, own = lax.optimization_barrier((gathered, child_rows, own))

    half_piece = jax.ShapeDtypeStruct((PANEL // 2, BLK), jnp.float32)
    lead_keep, lead_give = with_blocks(
        lead_part_kernel,
        5,
        [half_piece] * 2,
        (where[:5], there[:5], place),
        (inv_high, inv_low, own),
        gathered,
    )
    lead_got = swap_core(lead_give)
    wide = jax.ShapeDtypeStruct((PIV, PANEL), jnp.bfloat16)
    solved = with_blocks(
        solved_kernel, 4, [wide, wide], (where[5:9], there[5:9]), (inv_high, inv_low), gathered
    )

    half_top = jax.ShapeDtypeStruct((4, BLK, PANEL), jnp.float32)
    top_keep, top_give = with_blocks(
        top_kernel,
        8,
        [half_top] * 2,
        (where[9:], there[9:], spot[9:], place),
        (*solved, parent_matrix),
        gathered,
    )
    top_got = swap_core(top_give)
    lead_mine = after(lead_keep + lead_got, top_give)
    others = [along_z(lead_mine, s) for s in (1, 2, 3)]
    top_mine = top_keep + top_got
    strips = [along_z(top_mine[s], s) for s in (1, 2, 3)]
    lead_mine = lead_mine + others[0] + others[1] + others[2]
    lead_other = swap_core(lead_mine)
    lead_near = (
        jnp.stack(fetch(lead_mine, along_y)),
        jnp.stack(fetch(lead_other, along_x)),
    )
    strip = top_mine[0] + strips[0] + strips[1] + strips[2]
    turn = [
        (gg * 16 + cc, (cc // 2) * 16 + 2 * gg + cc % 2) for gg in range(8) for cc in range(16)
    ]
    turned = lax.ppermute(strip, ("grp", "col"), turn)
    top_all = lax.all_gather(strip, "grp", axis=0)

    slab_all = schur_slab(mapping, absent, after(gathered, strip), *solved)
    update = lax.psum_scatter(slab_all, "grp", scatter_dimension=0, tiled=True)

    lead_far = plane_far(lead_near)
    turned, _, top_all = lax.optimization_barrier((turned, slab_all, top_all))
    row_near = plane_near(turned)
    inv, low_first = lead_start(place, lead_far, 4)
    row_far = plane_far(row_near)
    inv, low_second = lead_next(inv, 4, 8)

    change = solve(place, inv, low_first, low_second, top_all, row_far)

    below = (g > 0) & (c >= 2)
    keep_first = below | (at_top & (c > 0))
    keep_second = c >= 2
    kept = jnp.where(jnp.arange(LEAD)[:, None] < PANEL, keep_first, keep_second)
    base = jnp.where(kept, parent_matrix, 0.0) - change
    matrix = lax.optimization_barrier(base) + jnp.where(kept, update, 0.0)
    return (child_rows[None], matrix)


def solution(mesh):
    return jax.shard_map(
        program,
        mesh=mesh,
        in_specs=(P("grp", None, None), P("grp", "col", None), P(), P("grp", "col")),
        out_specs=(P("grp", "col", None), P("grp", "col")),
        check_vma=False,
    )
```

```python
import functools

import jax
import jax.numpy as jnp
from jax import lax
from jax.experimental import pallas as pl
from jax.experimental.pallas import tpu as pltpu
from jax.sharding import PartitionSpec as P


BLK = 128
PANEL = 512
LEAD = 1024
PIV = 1024
SBLK = 32
PBLK = 64
PACK = 64

HIGHEST = lax.Precision.HIGHEST


def eliminate(work):
    order = BLK
    lane = lax.broadcasted_iota(jnp.int32, (8, order), 1)
    sub = lax.broadcasted_iota(jnp.int32, (8, order), 0)
    parts = order // 8
    rows = [work[8 * q : 8 * q + 8, :] for q in range(parts)]
    low = [jnp.zeros((8, order), jnp.float32) for _ in range(parts)]
    for q in range(parts):
        cols = [
            [
                jnp.broadcast_to(rows[p][:, 8 * q + k : 8 * q + k + 1], (8, order))
                for p in range(q, parts)
            ]
            for k in range(8)
        ]
        here = (lane >= 8 * q) & (lane < 8 * q + 8)
        mine = jnp.where(here, jnp.where(lane == sub + 8 * q, 1.0, 0.0), rows[q])
        fresh = []
        for k in range(8):
            raw = cols[k]
            root = lax.rsqrt(jnp.broadcast_to(raw[0][k : k + 1, :], (8, order)))
            scales = [jnp.broadcast_to(raw[0][m : m + 1, :], (8, order)) for m in range(k + 1, 8)]
            row = jnp.broadcast_to(mine[k : k + 1, :], (8, order)) * root
            fresh.append(row)
            done = [c * root for c in raw]
            for m in range(k + 1, 8):
                scale = scales[m - k - 1] * root
                cols[m] = [a - b * scale for a, b in zip(cols[m], done)]
            mine = jnp.where(sub > k, mine - done[0] * row, jnp.where(sub == k, row, mine))
            cols[k] = [jnp.where(sub >= k, done[0], 0.0)] + done[1:]
        rows[q] = mine
        for p in range(q, parts):
            for k in range(8):
                low[p] = jnp.where(lane == 8 * q + k, cols[k][p - q], low[p])
        for p in range(q + 1, parts):
            acc = jnp.where(here, 0.0, rows[p])
            for k in range(8):
                acc = acc - cols[k][p - q] * fresh[k]
            rows[p] = acc
    for q in range(parts):
        rows[q] = jnp.where(lane <= sub + 8 * q, rows[q], 0.0)
    return jnp.concatenate(rows, axis=0), jnp.concatenate(low, axis=0)


def exact(a, b):
    return jnp.dot(a, b, precision=HIGHEST, preferred_element_type=jnp.float32)


def factor_steps(first, last, t_ref, l_ref, r_ref, terms=None):
    order = t_ref.shape[0]
    blocks = order // BLK

    def keep(rows):
        if terms is not None:
            terms[0][rows, :], terms[1][rows, :] = split(r_ref[rows, :])

    def change(left, rows):
        if terms is None:
            return exact(left, r_ref[rows, :])
        return product(split(left), (terms[0][rows, :], terms[1][rows, :]))

    def pair(p, carry):
        base = pl.multiple_of(p * 2 * BLK, 2 * BLK)
        out = pl.multiple_of(base - first * BLK, 2 * BLK)
        if l_ref is not None:
            l_ref[:, pl.ds(out, 2 * BLK)] = jnp.zeros((order, 2 * BLK), jnp.float32)

        def one(j, carry):
            at = pl.multiple_of(base + j * BLK, BLK)
            rows = pl.ds(pl.multiple_of(j * BLK, BLK), BLK)
            inv, low = eliminate(t_ref[pl.ds(at, BLK), pl.ds(at, BLK)])
            r_ref[rows, :] = exact(inv, t_ref[pl.ds(at, BLK), :])
            r_ref[rows, pl.ds(at, BLK)] = inv
            t_ref[pl.ds(at, BLK), :] = r_ref[rows, :]
            if l_ref is not None:
                to = pl.multiple_of(out + j * BLK, BLK)
                l_ref[pl.ds(at, BLK), pl.ds(to, BLK)] = low
            keep(rows)

            @pl.when(j == 0)
            def _():
                to = pl.multiple_of(base + BLK, BLK)
                top = slice(0, BLK)
                left = r_ref[top, pl.ds(to, BLK)].T
                if l_ref is not None:
                    l_ref[pl.ds(to, BLK), pl.ds(out, BLK)] = left
                t_ref[pl.ds(to, BLK), pl.ds(base, BLK)] = jnp.zeros((BLK, BLK), jnp.float32)
                t_ref[pl.ds(to, BLK), :] = t_ref[pl.ds(to, BLK), :] - change(left, top)
                r_ref[top, pl.ds(to, BLK)] = jnp.zeros((BLK, BLK), jnp.float32)
                keep(top)

            return carry

        lax.fori_loop(0, 2, one, 0)

        def below(i, carry):
            to = pl.multiple_of(i * BLK, BLK)
            left = r_ref[:, pl.ds(to, BLK)].T
            if l_ref is not None:
                l_ref[pl.ds(to, BLK), pl.ds(out, 2 * BLK)] = left
            t_ref[pl.ds(to, BLK), pl.ds(base, 2 * BLK)] = jnp.zeros((BLK, 2 * BLK), jnp.float32)
            t_ref[pl.ds(to, BLK), :] = t_ref[pl.ds(to, BLK), :] - change(left, slice(0, 2 * BLK))
            return carry

        return lax.fori_loop(2 * p + 2, blocks, below, carry)

    lax.fori_loop(first // 2, last // 2, pair, 0)
    if last == blocks:
        for b in range(blocks - 1):
            width = order - BLK * (b + 1)
            t_ref[BLK * b : BLK * b + BLK, BLK * (b + 1) :] = jnp.zeros((BLK, width), jnp.float32)


def child_kernel(a_ref, t_ref, r_ref):
    t_ref[...] = a_ref[...]
    factor_steps(0, PIV // BLK, t_ref, None, r_ref)


def lead_start_kernel(last, place_ref, *refs):
    pieces, (t_ref, l_ref, r_ref, *terms) = refs[:8], refs[8:]
    core, px, py = place_ref[3], place_ref[4], place_ref[5]
    half = PANEL // 2
    for sx in range(4):
        for sy in range(4):
            x, y = (px + 4 - sx) % 4, (py + 4 - sy) % 4
            where = x * 4 + y
            row = (where % 2) * PANEL
            column = pl.multiple_of((where // 2) * BLK, BLK)
            first = pl.multiple_of(row + core * half, half)
            second = pl.multiple_of(row + (1 - core) * half, half)
            to = pl.ds(column, BLK)
            for i in range(4):
                part = slice(i * BLK, i * BLK + BLK)
                t_ref[pl.ds(first + i * PACK, PACK), to] = pieces[sx][sy, :, part]
                t_ref[pl.ds(second + i * PACK, PACK), to] = pieces[4 + sy][sx, :, part]
    factor_steps(0, last, t_ref, l_ref, r_ref, terms)


def lead_next_kernel(first, last, t_in, t_ref, l_ref, r_ref, *terms):
    t_ref[...] = t_in[...]
    factor_steps(first, last, t_ref, l_ref, r_ref, terms)


WHOLE = pl.BlockSpec(memory_space=pltpu.VMEM)
TABLE = pl.BlockSpec(memory_space=pltpu.SMEM)


def square(order):
    return jax.ShapeDtypeStruct((order, order), jnp.float32)


def limit(mib):
    return pltpu.CompilerParams(vmem_limit_bytes=mib << 20)


def work(gflop, mib):
    return pl.CostEstimate(
        flops=int(gflop * 10**9), bytes_accessed=mib << 20, transcendentals=0
    )


def child_factor(matrix):
    return pl.pallas_call(
        child_kernel,
        out_shape=square(PIV),
        in_specs=[WHOLE],
        out_specs=WHOLE,
        scratch_shapes=[pltpu.VMEM((2 * BLK, PIV), jnp.float32)],
        cost_estimate=work(40, 12),
        compiler_params=limit(24),
        name="child_factor",
    )(matrix)


def lead_call(kernel, columns, in_specs):
    return pl.pallas_call(
        kernel,
        out_shape=[square(LEAD), jax.ShapeDtypeStruct((LEAD, columns), jnp.float32)],
        in_specs=in_specs,
        out_specs=[WHOLE] * 2,
        scratch_shapes=[pltpu.VMEM((2 * BLK, LEAD), jnp.float32)]
        + [pltpu.VMEM((2 * BLK, LEAD), jnp.bfloat16)] * 2,
        cost_estimate=work(10, 12),
        compiler_params=limit(24),
    )


def lead_start(place, pieces, last):
    kernel = functools.partial(lead_start_kernel, last)
    return lead_call(kernel, last * BLK, [TABLE] + [WHOLE] * 8)(place, *pieces)


def lead_next(t, first, last):
    kernel = functools.partial(lead_next_kernel, first, last)
    return lead_call(kernel, (last - first) * BLK, [WHOLE])(t)


def split(x):
    high = x.astype(jnp.bfloat16)
    return high, (x - high.astype(jnp.float32)).astype(jnp.bfloat16)


def product(a, b, turned=False):
    dims = (((1,), (1 if turned else 0,)), ((), ()))

    def one(x, y):
        return lax.dot_general(x, y, dims, preferred_element_type=jnp.float32)

    return one(a[0], b[0]) + one(a[0], b[1]) + one(a[1], b[0])


def each(count, body, width=256):
    def one(i, carry):
        body(pl.ds(pl.multiple_of(i * width, width), width))
        return carry

    lax.fori_loop(0, count, one, 0)


def rows_kernel(t_ref, c_ref, high_ref, low_ref, out_ref, sh, sl):
    high_ref[...], low_ref[...] = split(t_ref[...])
    sh[...], sl[...] = split(c_ref[...])

    def body(at):
        inverse = (high_ref[at, :], low_ref[at, :])
        out_ref[:, at] = product((sh[...], sl[...]), inverse, True)

    each(PIV // 256, body)


def child_rows_of(inverse, rows):
    half = jax.ShapeDtypeStruct((PIV, PIV), jnp.bfloat16)
    return pl.pallas_call(
        rows_kernel,
        out_shape=[half, half, jax.ShapeDtypeStruct(rows.shape, jnp.float32)],
        in_specs=[WHOLE] * 2,
        out_specs=[WHOLE] * 3,
        scratch_shapes=[pltpu.VMEM(rows.shape, jnp.bfloat16)] * 2,
        cost_estimate=work(2, 10),
        compiler_params=limit(32),
        name="child_rows",
    )(inverse, rows)


def load_blocks(count, where_ref, there_ref, rows_ref, got, sem):
    def copy(i):
        start = pl.multiple_of(where_ref[i] * BLK, BLK)
        return pltpu.make_async_copy(
            rows_ref.at[pl.ds(start, BLK)], got.at[pl.ds(i * BLK, BLK)], sem.at[i]
        )

    for i in range(count):
        copy(i).start()
    for i in range(count):
        copy(i).wait()

        @pl.when(there_ref[i] == 0)
        def _():
            got[i * BLK : i * BLK + BLK, :] = jnp.zeros((BLK, PIV), jnp.float32)


def lead_part_kernel(
    where_ref, there_ref, place_ref, high_ref, low_ref, own_ref, rows_ref, keep_ref, give_ref, got, sem
):
    load_blocks(5, where_ref, there_ref, rows_ref, got, sem)
    core = place_ref[3]
    half = PANEL // 2
    inverse = (high_ref[...], low_ref[...])
    half_way = product(split(got[4 * BLK :, :]), inverse, True)
    solved = product(split(half_way), inverse)
    part = product(split(got[: 4 * BLK, :]), split(solved), True)
    keep = own_ref[pl.ds(pl.multiple_of(core * half, half), half), :] - part[:half]
    give = own_ref[pl.ds(pl.multiple_of((1 - core) * half, half), half), :] - part[half:]
    for i in range(4):
        keep_ref[:, i * BLK : i * BLK + BLK] = keep[i * PACK : i * PACK + PACK]
        give_ref[:, i * BLK : i * BLK + BLK] = give[i * PACK : i * PACK + PACK]


def top_kernel(
    where_ref, there_ref, spot_ref, place_ref, high_ref, low_ref, own_ref, lead_keep_ref, lead_give_ref, rows_ref, keep_ref, give_ref, got, sem
):
    load_blocks(8, where_ref, there_ref, rows_ref, got, sem)
    solved = (high_ref[...], low_ref[...])
    at_top = place_ref[0] == 0
    keep_ref[PANEL:, :] = lead_keep_ref[...]
    give_ref[PANEL:, :] = lead_give_ref[...]
    for half, out_ref in ((0, keep_ref), (1, give_ref)):
        part = product(split(got[half * PANEL : half * PANEL + PANEL, :]), solved)
        for i in range(4):
            at = pl.multiple_of(spot_ref[half * 4 + i] * BLK, BLK)
            own = jnp.where(at_top, own_ref[pl.ds(at, BLK), :], 0.0)
            out_ref[i * BLK : i * BLK + BLK, :] = part[i * BLK : i * BLK + BLK] + own


def solved_kernel(where_ref, there_ref, high_ref, low_ref, rows_ref, oh_ref, ol_ref, got, sem):
    load_blocks(4, where_ref, there_ref, rows_ref, got, sem)
    inverse = (high_ref[...], low_ref[...])
    half_way = product(split(got[...]), inverse, True)
    solved = product(split(half_way), inverse)
    oh_ref[...], ol_ref[...] = split(-solved.T)


def with_blocks(kernel, count, out_shape, tables, inputs, rows):
    return pl.pallas_call(
        kernel,
        out_shape=out_shape,
        in_specs=[TABLE] * len(tables)
        + [WHOLE] * len(inputs)
        + [pl.BlockSpec(memory_space=pl.ANY)],
        out_specs=[WHOLE] * len(out_shape),
        scratch_shapes=[
            pltpu.VMEM((count * BLK, PIV), jnp.float32),
            pltpu.SemaphoreType.DMA((count,)),
        ],
        cost_estimate=work(3, 8),
        compiler_params=limit(40),
    )(*tables, *inputs, rows)


def solve_kernel(
    place_ref, t_ref, first_ref, second_ref, top_ref, *refs
):
    pieces, (out_ref, th, tl, uh, ul, ph, pl_, fh, fl, xh, xl, rh, rl) = refs[:8], refs[8:]
    g, c, px, py = place_ref[0], place_ref[1], place_ref[4], place_ref[5]
    half = PANEL

    th[...], tl[...] = split(t_ref[...])
    for i in range(4):
        for j in range(4):
            rows = slice(256 * j, 256 * j + 256)
            cols = slice(256 * i, 256 * i + 256)
            uh[rows, cols], ul[rows, cols] = split(t_ref[cols, rows].T)
    for source in range(8):
        start = (source % 2 * 4 + source // 2) * BLK
        at = slice(start, start + BLK)
        ph[at, :], pl_[at, :] = split(top_ref[source])

    for i in range(4):
        at, upto = slice(256 * i, 256 * i + 256), slice(0, 256 * i + 256)
        x = product((th[at, upto], tl[at, upto]), (ph[upto, :], pl_[upto, :]))
        fh[at, :], fl[at, :] = split(x)

    @pl.when(g == 0)
    def _():
        @pl.when(c == 0)
        def _():
            out_ref[...] = -first_ref[...]

        @pl.when(c == 1)
        def _():
            out_ref[:half, :] = jnp.zeros((half, half), jnp.float32)
            out_ref[half:, :] = -second_ref[half:, :]

        @pl.when(c >= 2)
        def _():
            out_ref[:half, :] = jnp.zeros((half, half), jnp.float32)
            left = split(first_ref[half:, :])
            out_ref[half:, :] = product(left, (fh[:half, :], fl[:half, :]))

    @pl.when(g > 0)
    def _():
        @pl.when(c == 0)
        def _():
            xh[...], xl[...] = -uh[:, :half], -ul[:, :half]

        @pl.when(c == 1)
        def _():
            xh[...], xl[...] = -uh[:, half:], -ul[:, half:]

        @pl.when(c >= 2)
        def _():
            for i in range(4):
                at, since = slice(256 * i, 256 * i + 256), slice(256 * i, LEAD)
                x = product((uh[at, since], ul[at, since]), (fh[since, :], fl[since, :]))
                xh[at, :], xl[at, :] = split(x)

        for sx in range(4):
            for sy in range(4):
                x, y = (px + 4 - sx) % 4, (py + 4 - sy) % 4
                where = x * 4 + y
                source = where // 2
                row = pl.multiple_of((where % 2) * half, half)
                column = pl.multiple_of(((source % 2) * 4 + source // 2) * BLK, BLK)
                tile = jnp.concatenate([pieces[sx][sy], pieces[4 + sy][sx]], axis=0).T
                to = (pl.ds(row, half), pl.ds(column, BLK))
                rh[to], rl[to] = split(tile)

        def update(at):
            out_ref[at, :] = product((rh[at, :], rl[at, :]), (xh[...], xl[...]))

        each(4, update)


def solve(place, inverse, first, second, top, pieces):
    def pair(rows, cols):
        return [pltpu.VMEM((rows, cols), jnp.bfloat16)] * 2

    return pl.pallas_call(
        solve_kernel,
        out_shape=jax.ShapeDtypeStruct((LEAD, PANEL), jnp.float32),
        in_specs=[TABLE] + [WHOLE] * 12,
        out_specs=WHOLE,
        scratch_shapes=pair(LEAD, LEAD) * 2 + pair(LEAD, PANEL) * 3 + pair(LEAD, LEAD),
        cost_estimate=work(10, 20),
        compiler_params=limit(36),
        name="solve",
    )(place, inverse, first, second, top, *pieces)


def schur_kernel(step_blocks, present_ref, absent_ref, rows_ref, high_ref, low_ref, out_ref, buf, zero, sem, zsem):
    step = pl.program_id(0)
    steps = pl.num_programs(0)
    slot = lax.rem(step, 2)

    def put(which, index, to):
        return pltpu.make_async_copy(
            buf.at[which, pl.ds(index * BLK, BLK)],
            out_ref.at[pl.ds(pl.multiple_of(to * BLK, BLK), BLK)],
            sem.at[which, index],
        )

    def clear(index, to):
        return pltpu.make_async_copy(
            zero, out_ref.at[pl.ds(pl.multiple_of(to * BLK, BLK), BLK)], zsem.at[index]
        )

    @pl.when(step == 0)
    def _():
        zero[...] = jnp.zeros_like(zero)

    for i in range(step_blocks):
        clear(i, absent_ref[step * step_blocks + i]).start()
    x = rows_ref[...]
    xh = x.astype(jnp.bfloat16)
    xl = (x - xh.astype(jnp.float32)).astype(jnp.bfloat16)
    wh = high_ref[...]
    total = jnp.dot(xh, wh, preferred_element_type=jnp.float32)
    total += jnp.dot(xh, low_ref[...], preferred_element_type=jnp.float32)
    total += jnp.dot(xl, wh, preferred_element_type=jnp.float32)

    @pl.when(step >= 2)
    def _():
        for i in range(step_blocks):
            put(slot, i, 0).wait()

    buf[slot] = total
    for i in range(step_blocks):
        put(slot, i, present_ref[step * step_blocks + i]).start()
    for i in range(step_blocks):
        clear(i, 0).wait()

    @pl.when(step == steps - 1)
    def _():
        for i in range(step_blocks):
            put(slot, i, 0).wait()
            put(1 - slot, i, 0).wait()


def schur_slab(present, absent, rows, high, low, step_blocks=4):
    width = high.shape[1]
    steps = SBLK // step_blocks
    return pl.pallas_call(
        functools.partial(schur_kernel, step_blocks),
        out_shape=jax.ShapeDtypeStruct((PBLK * BLK, width), jnp.float32),
        grid_spec=pltpu.PrefetchScalarGridSpec(
            num_scalar_prefetch=2,
            grid=(steps,),
            in_specs=[
                pl.BlockSpec((step_blocks * BLK, PIV), lambda i, p, a: (i, 0)),
                pl.BlockSpec((PIV, width), lambda i, p, a: (0, 0)),
                pl.BlockSpec((PIV, width), lambda i, p, a: (0, 0)),
            ],
            out_specs=pl.BlockSpec(memory_space=pltpu.HBM),
            scratch_shapes=[
                pltpu.VMEM((2, step_blocks * BLK, width), jnp.float32),
                pltpu.VMEM((BLK, width), jnp.float32),
                pltpu.SemaphoreType.DMA((2, step_blocks)),
                pltpu.SemaphoreType.DMA((step_blocks,)),
            ],
        ),
        cost_estimate=pl.CostEstimate(
            flops=6 * SBLK * BLK * PIV * width, bytes_accessed=36 << 20, transcendentals=0
        ),
        compiler_params=pltpu.CompilerParams(
            dimension_semantics=("arbitrary",), vmem_limit_bytes=58 << 20
        ),
        name="schur",
    )(present, absent, rows, high, low)


def swap_core(x):
    return lax.ppermute(x, "grp", [(i, i ^ 1) for i in range(8)])


def along_z(x, shift):
    return lax.ppermute(x, "grp", [(i, (i + 2 * shift) % 8) for i in range(8)])


def along_x(x, shift):
    return lax.ppermute(x, "col", [(i, (i + 4 * shift) % 16) for i in range(16)])


def along_y(x, shift):
    return lax.ppermute(x, "col", [(i, i // 4 * 4 + (i + shift) % 4) for i in range(16)])


def fetch(x, mover):
    return [x] + [mover(x, s) for s in (1, 2, 3)]


def plane_near(x):
    half = x.shape[0] // 2
    return jnp.stack(fetch(x[:half], along_y)), jnp.stack(fetch(x[half:], along_x))


def plane_far(near):
    return fetch(near[0], along_x) + fetch(near[1], along_y)


def pick(x, index, axis):
    return lax.dynamic_index_in_dim(x, index, axis, keepdims=False)


def after(value, *others):
    return lax.optimization_barrier((value, *others))[0]


def program(pivot_blocks, coupling, block_map, parent_matrix):
    g = lax.axis_index("grp")
    c = lax.axis_index("col")
    pz, core = g // 2, g % 2
    px, py = c // 4, c % 4
    at_top = g == 0
    place = jnp.stack([g, c, pz, core, px, py]).astype(jnp.int32)

    gathered = lax.all_gather(coupling[0], "col", axis=0, tiled=True)

    lead_own = []
    for s in range(8):
        row, column = PANEL * (s % 2), BLK * (s // 2)
        piece = parent_matrix[row : row + PANEL, column : column + BLK]
        lead_own.append(lax.ppermute(piece, ("grp", "col"), [(0, s), (1, 8 + s)]))

    mapping = pick(block_map, g, 0)
    spots = jnp.arange(PBLK, dtype=jnp.int32)
    matches = mapping[None, :] == spots[:, None]
    position = jnp.sum(jnp.where(matches, jnp.arange(SBLK, dtype=jnp.int32)[None, :], 0), axis=1)
    present = jnp.any(matches, axis=1)
    rank = jnp.sum((spots[None, :] < spots[:, None]) & ~present[None, :], axis=1)
    slots = jnp.arange(SBLK, dtype=jnp.int32)
    absent = jnp.sum(
        jnp.where((rank[None, :] == slots[:, None]) & ~present[None, :], spots[None, :], 0), axis=1
    ).astype(jnp.int32)
    n = jnp.arange(17, dtype=jnp.int32)
    side = jnp.where(n % 4 < 2, core, 1 - core)
    lead_spot = 4 * (c % 2) + 2 * side + n % 2
    top_side = jnp.where(n < 13, core, 1 - core)
    top_spot = 4 * top_side + (pz + n - 9) % 4
    spot = jnp.where(
        n < 4, lead_spot, jnp.where(n < 5, c // 2, jnp.where(n < 9, 4 * c + n - 5, top_spot))
    ).astype(jnp.int32)
    chosen = spot[:, None] == spots[None, :]
    where = jnp.sum(jnp.where(chosen, position[None, :], 0), axis=1)
    there = jnp.sum((chosen & present[None, :]).astype(jnp.int32), axis=1)

    pivot, mapping, where, there, absent, place, spot = lax.optimization_barrier(
        (pivot_blocks[0], mapping, where, there, absent, place, spot)
    )
    child_inv = child_factor(pivot)
    inv_high, inv_low, child_rows = child_rows_of(child_inv, coupling[0])
    own = lead_own[0]
    for more in lead_own[1:]:
        own = own + more
    gathered, child_rows, own = lax.optimization_barrier((gathered, child_rows, own))

    half_piece = jax.ShapeDtypeStruct((PACK, PANEL), jnp.float32)
    lead_keep, lead_give = with_blocks(
        lead_part_kernel,
        5,
        [half_piece] * 2,
        (where[:5], there[:5], place),
        (inv_high, inv_low, own),
        gathered,
    )
    wide = jax.ShapeDtypeStruct((PIV, PANEL), jnp.bfloat16)
    solved = with_blocks(
        solved_kernel,
        4,
        [wide, wide],
        (where[5:9], there[5:9]),
        (inv_high, inv_low),
        after(gathered, lead_keep),
    )

    half_top = jax.ShapeDtypeStruct((PANEL + PACK, PANEL), jnp.float32)
    top_keep, top_give = with_blocks(
        top_kernel,
        8,
        [half_top] * 2,
        (where[9:], there[9:], spot[9:], place),
        (*solved, parent_matrix, lead_keep, lead_give),
        gathered,
    )
    mine = top_keep + swap_core(top_give)

    def parcel(i):
        return jnp.concatenate([mine[i * BLK : i * BLK + BLK], mine[PANEL:]], axis=0)

    got = [along_z(parcel(i), i) for i in (1, 2, 3)]
    total = parcel(0) + got[0] + got[1] + got[2]
    strip, lead_mine = total[:BLK], total[BLK:]
    turn = [
        (gg * 16 + cc, (cc // 2) * 16 + 2 * gg + cc % 2) for gg in range(8) for cc in range(16)
    ]
    turned = lax.ppermute(strip, ("grp", "col"), turn)
    top_all = lax.all_gather(strip, "grp", axis=0)

    slab_all = schur_slab(mapping, absent, gathered, *solved)
    update = lax.psum_scatter(slab_all, "grp", scatter_dimension=0, tiled=True)

    lead_other = swap_core(lead_mine)
    lead_near = (
        jnp.stack(fetch(lead_mine, along_y)),
        jnp.stack(fetch(lead_other, along_x)),
    )
    lead_far = plane_far(lead_near)
    turned, _, top_all = lax.optimization_barrier((turned, slab_all, top_all))
    row_near = plane_near(turned)
    inv, low_first = lead_start(place, lead_far, 4)
    row_far = plane_far(row_near)
    inv, low_second = lead_next(inv, 4, 8)

    change = solve(place, inv, low_first, low_second, top_all, row_far)

    below = (g > 0) & (c >= 2)
    keep_first = below | (at_top & (c > 0))
    keep_second = c >= 2
    kept = jnp.where(jnp.arange(LEAD)[:, None] < PANEL, keep_first, keep_second)
    base = jnp.where(kept, parent_matrix, 0.0) - change
    matrix = lax.optimization_barrier(base) + jnp.where(kept, update, 0.0)
    return (child_rows[None], matrix)


def solution(mesh):
    return jax.shard_map(
        program,
        mesh=mesh,
        in_specs=(P("grp", None, None), P("grp", "col", None), P(), P("grp", "col")),
        out_specs=(P("grp", "col", None), P("grp", "col")),
        check_vma=False,
    )
```

```python
import functools

import jax
import jax.numpy as jnp
from jax import lax
from jax.experimental import pallas as pl
from jax.experimental.pallas import tpu as pltpu
from jax.sharding import PartitionSpec as P


BLK = 128
PANEL = 512
LEAD = 1024
PIV = 1024
SBLK = 32
PBLK = 64

HIGHEST = lax.Precision.HIGHEST


def eliminate(work):
    order = BLK
    lane = lax.broadcasted_iota(jnp.int32, (8, order), 1)
    sub = lax.broadcasted_iota(jnp.int32, (8, order), 0)
    parts = order // 8
    rows = [work[8 * q : 8 * q + 8, :] for q in range(parts)]
    low = [jnp.zeros((8, order), jnp.float32) for _ in range(parts)]
    for q in range(parts):
        cols = [
            [
                jnp.broadcast_to(rows[p][:, 8 * q + k : 8 * q + k + 1], (8, order))
                for p in range(q, parts)
            ]
            for k in range(8)
        ]
        here = (lane >= 8 * q) & (lane < 8 * q + 8)
        mine = jnp.where(here, jnp.where(lane == sub + 8 * q, 1.0, 0.0), rows[q])
        fresh = []
        for k in range(8):
            raw = cols[k]
            root = lax.rsqrt(jnp.broadcast_to(raw[0][k : k + 1, :], (8, order)))
            scales = [jnp.broadcast_to(raw[0][m : m + 1, :], (8, order)) for m in range(k + 1, 8)]
            row = jnp.broadcast_to(mine[k : k + 1, :], (8, order)) * root
            fresh.append(row)
            done = [c * root for c in raw]
            for m in range(k + 1, 8):
                scale = scales[m - k - 1] * root
                cols[m] = [a - b * scale for a, b in zip(cols[m], done)]
            mine = jnp.where(sub > k, mine - done[0] * row, jnp.where(sub == k, row, mine))
            cols[k] = [jnp.where(sub >= k, done[0], 0.0)] + done[1:]
        rows[q] = mine
        for p in range(q, parts):
            for k in range(8):
                low[p] = jnp.where(lane == 8 * q + k, cols[k][p - q], low[p])
        for p in range(q + 1, parts):
            acc = jnp.where(here, 0.0, rows[p])
            for k in range(8):
                acc = acc - cols[k][p - q] * fresh[k]
            rows[p] = acc
    for q in range(parts):
        rows[q] = jnp.where(lane <= sub + 8 * q, rows[q], 0.0)
    return jnp.concatenate(rows, axis=0), jnp.concatenate(low, axis=0)


def exact(a, b):
    return jnp.dot(a, b, precision=HIGHEST, preferred_element_type=jnp.float32)


def factor_steps(first, last, t_ref, l_ref, r_ref, terms=None):
    order = t_ref.shape[0]
    blocks = order // BLK

    def keep(rows):
        if terms is not None:
            terms[0][rows, :], terms[1][rows, :] = split(r_ref[rows, :])

    def change(left, rows):
        if terms is None:
            return exact(left, r_ref[rows, :])
        return product(split(left), (terms[0][rows, :], terms[1][rows, :]))

    def pair(p, carry):
        base = pl.multiple_of(p * 2 * BLK, 2 * BLK)
        out = pl.multiple_of(base - first * BLK, 2 * BLK)
        if l_ref is not None:
            l_ref[:, pl.ds(out, 2 * BLK)] = jnp.zeros((order, 2 * BLK), jnp.float32)

        def one(j, carry):
            at = pl.multiple_of(base + j * BLK, BLK)
            rows = pl.ds(pl.multiple_of(j * BLK, BLK), BLK)
            inv, low = eliminate(t_ref[pl.ds(at, BLK), pl.ds(at, BLK)])
            r_ref[rows, :] = exact(inv, t_ref[pl.ds(at, BLK), :])
            r_ref[rows, pl.ds(at, BLK)] = inv
            t_ref[pl.ds(at, BLK), :] = r_ref[rows, :]
            if l_ref is not None:
                to = pl.multiple_of(out + j * BLK, BLK)
                l_ref[pl.ds(at, BLK), pl.ds(to, BLK)] = low
            keep(rows)

            @pl.when(j == 0)
            def _():
                to = pl.multiple_of(base + BLK, BLK)
                top = slice(0, BLK)
                left = r_ref[top, pl.ds(to, BLK)].T
                if l_ref is not None:
                    l_ref[pl.ds(to, BLK), pl.ds(out, BLK)] = left
                t_ref[pl.ds(to, BLK), pl.ds(base, BLK)] = jnp.zeros((BLK, BLK), jnp.float32)
                t_ref[pl.ds(to, BLK), :] = t_ref[pl.ds(to, BLK), :] - change(left, top)
                r_ref[top, pl.ds(to, BLK)] = jnp.zeros((BLK, BLK), jnp.float32)
                keep(top)

            return carry

        lax.fori_loop(0, 2, one, 0)

        def below(i, carry):
            to = pl.multiple_of(i * BLK, BLK)
            left = r_ref[:, pl.ds(to, BLK)].T
            if l_ref is not None:
                l_ref[pl.ds(to, BLK), pl.ds(out, 2 * BLK)] = left
            t_ref[pl.ds(to, BLK), pl.ds(base, 2 * BLK)] = jnp.zeros((BLK, 2 * BLK), jnp.float32)
            t_ref[pl.ds(to, BLK), :] = t_ref[pl.ds(to, BLK), :] - change(left, slice(0, 2 * BLK))
            return carry

        return lax.fori_loop(2 * p + 2, blocks, below, carry)

    lax.fori_loop(first // 2, last // 2, pair, 0)
    if last == blocks:
        for b in range(blocks - 1):
            width = order - BLK * (b + 1)
            t_ref[BLK * b : BLK * b + BLK, BLK * (b + 1) :] = jnp.zeros((BLK, width), jnp.float32)


def child_kernel(a_ref, t_ref, r_ref):
    t_ref[...] = a_ref[...]
    factor_steps(0, PIV // BLK, t_ref, None, r_ref)


def lead_start_kernel(last, place_ref, *refs):
    pieces, (t_ref, l_ref, r_ref, *terms) = refs[:8], refs[8:]
    core, px, py = place_ref[3], place_ref[4], place_ref[5]
    half = PANEL // 2
    for sx in range(4):
        for sy in range(4):
            x, y = (px + 4 - sx) % 4, (py + 4 - sy) % 4
            where = x * 4 + y
            row = (where % 2) * PANEL
            column = pl.multiple_of((where // 2) * BLK, BLK)
            first = pl.multiple_of(row + core * half, half)
            second = pl.multiple_of(row + (1 - core) * half, half)
            t_ref[pl.ds(first, half), pl.ds(column, BLK)] = pieces[sx][sy]
            t_ref[pl.ds(second, half), pl.ds(column, BLK)] = pieces[4 + sy][sx]
    factor_steps(0, last, t_ref, l_ref, r_ref, terms)


def lead_next_kernel(first, last, t_in, t_ref, l_ref, r_ref, *terms):
    t_ref[...] = t_in[...]
    factor_steps(first, last, t_ref, l_ref, r_ref, terms)


WHOLE = pl.BlockSpec(memory_space=pltpu.VMEM)
TABLE = pl.BlockSpec(memory_space=pltpu.SMEM)


def square(order):
    return jax.ShapeDtypeStruct((order, order), jnp.float32)


def limit(mib):
    return pltpu.CompilerParams(vmem_limit_bytes=mib << 20)


def work(gflop, mib):
    return pl.CostEstimate(
        flops=int(gflop * 10**9), bytes_accessed=mib << 20, transcendentals=0
    )


def child_factor(matrix):
    return pl.pallas_call(
        child_kernel,
        out_shape=square(PIV),
        in_specs=[WHOLE],
        out_specs=WHOLE,
        scratch_shapes=[pltpu.VMEM((2 * BLK, PIV), jnp.float32)],
        cost_estimate=work(40, 12),
        compiler_params=limit(24),
        name="child_factor",
    )(matrix)


def lead_call(kernel, columns, in_specs):
    return pl.pallas_call(
        kernel,
        out_shape=[square(LEAD), jax.ShapeDtypeStruct((LEAD, columns), jnp.float32)],
        in_specs=in_specs,
        out_specs=[WHOLE] * 2,
        scratch_shapes=[pltpu.VMEM((2 * BLK, LEAD), jnp.float32)]
        + [pltpu.VMEM((2 * BLK, LEAD), jnp.bfloat16)] * 2,
        cost_estimate=work(10, 12),
        compiler_params=limit(24),
    )


def lead_start(place, pieces, last):
    kernel = functools.partial(lead_start_kernel, last)
    return lead_call(kernel, last * BLK, [TABLE] + [WHOLE] * 8)(place, *pieces)


def lead_next(t, first, last):
    kernel = functools.partial(lead_next_kernel, first, last)
    return lead_call(kernel, (last - first) * BLK, [WHOLE])(t)


def split(x):
    high = x.astype(jnp.bfloat16)
    return high, (x - high.astype(jnp.float32)).astype(jnp.bfloat16)


def product(a, b, turned=False):
    dims = (((1,), (1 if turned else 0,)), ((), ()))

    def one(x, y):
        return lax.dot_general(x, y, dims, preferred_element_type=jnp.float32)

    return one(a[0], b[0]) + one(a[0], b[1]) + one(a[1], b[0])


def each(count, body, width=256):
    def one(i, carry):
        body(pl.ds(pl.multiple_of(i * width, width), width))
        return carry

    lax.fori_loop(0, count, one, 0)


def rows_kernel(t_ref, c_ref, high_ref, low_ref, out_ref, sh, sl):
    high_ref[...], low_ref[...] = split(t_ref[...])
    sh[...], sl[...] = split(c_ref[...])

    def body(at):
        inverse = (high_ref[at, :], low_ref[at, :])
        out_ref[:, at] = product((sh[...], sl[...]), inverse, True)

    each(PIV // 256, body)


def child_rows_of(inverse, rows):
    half = jax.ShapeDtypeStruct((PIV, PIV), jnp.bfloat16)
    return pl.pallas_call(
        rows_kernel,
        out_shape=[half, half, jax.ShapeDtypeStruct(rows.shape, jnp.float32)],
        in_specs=[WHOLE] * 2,
        out_specs=[WHOLE] * 3,
        scratch_shapes=[pltpu.VMEM(rows.shape, jnp.bfloat16)] * 2,
        cost_estimate=work(2, 10),
        compiler_params=limit(32),
        name="child_rows",
    )(inverse, rows)


def load_blocks(count, where_ref, there_ref, rows_ref, got, sem):
    def copy(i):
        start = pl.multiple_of(where_ref[i] * BLK, BLK)
        return pltpu.make_async_copy(
            rows_ref.at[pl.ds(start, BLK)], got.at[pl.ds(i * BLK, BLK)], sem.at[i]
        )

    for i in range(count):
        copy(i).start()
    for i in range(count):
        copy(i).wait()

        @pl.when(there_ref[i] == 0)
        def _():
            got[i * BLK : i * BLK + BLK, :] = jnp.zeros((BLK, PIV), jnp.float32)


def lead_part_kernel(
    where_ref, there_ref, place_ref, high_ref, low_ref, own_ref, rows_ref, keep_ref, give_ref, got, sem
):
    load_blocks(5, where_ref, there_ref, rows_ref, got, sem)
    core = place_ref[3]
    half = PANEL // 2
    inverse = (high_ref[...], low_ref[...])
    half_way = product(split(got[4 * BLK :, :]), inverse, True)
    solved = product(split(half_way), inverse)
    part = product(split(got[: 4 * BLK, :]), split(solved), True)
    keep_ref[...] = own_ref[pl.ds(pl.multiple_of(core * half, half), half), :] - part[:half]
    give_ref[...] = own_ref[pl.ds(pl.multiple_of((1 - core) * half, half), half), :] - part[half:]


def top_kernel(
    where_ref, there_ref, spot_ref, place_ref, high_ref, low_ref, own_ref, rows_ref, keep_ref, give_ref, got, sem
):
    load_blocks(8, where_ref, there_ref, rows_ref, got, sem)
    solved = (high_ref[...], low_ref[...])
    at_top = place_ref[0] == 0
    for half, out_ref in ((0, keep_ref), (1, give_ref)):
        part = product(split(got[half * PANEL : half * PANEL + PANEL, :]), solved)
        for i in range(4):
            at = pl.multiple_of(spot_ref[half * 4 + i] * BLK, BLK)
            own = jnp.where(at_top, own_ref[pl.ds(at, BLK), :], 0.0)
            out_ref[i] = part[i * BLK : i * BLK + BLK] + own


def solved_kernel(where_ref, there_ref, high_ref, low_ref, rows_ref, oh_ref, ol_ref, got, sem):
    load_blocks(4, where_ref, there_ref, rows_ref, got, sem)
    inverse = (high_ref[...], low_ref[...])
    half_way = product(split(got[...]), inverse, True)
    solved = product(split(half_way), inverse)
    oh_ref[...], ol_ref[...] = split(-solved.T)


def with_blocks(kernel, count, out_shape, tables, inputs, rows):
    return pl.pallas_call(
        kernel,
        out_shape=out_shape,
        in_specs=[TABLE] * len(tables)
        + [WHOLE] * len(inputs)
        + [pl.BlockSpec(memory_space=pl.ANY)],
        out_specs=[WHOLE] * len(out_shape),
        scratch_shapes=[
            pltpu.VMEM((count * BLK, PIV), jnp.float32),
            pltpu.SemaphoreType.DMA((count,)),
        ],
        cost_estimate=work(3, 8),
        compiler_params=limit(40),
    )(*tables, *inputs, rows)


def solve_kernel(
    place_ref, t_ref, first_ref, second_ref, top_ref, *refs
):
    pieces, (out_ref, th, tl, uh, ul, ph, pl_, fh, fl, xh, xl, rh, rl) = refs[:8], refs[8:]
    g, c, px, py = place_ref[0], place_ref[1], place_ref[4], place_ref[5]
    half = PANEL

    th[...], tl[...] = split(t_ref[...])
    for i in range(4):
        for j in range(4):
            rows = slice(256 * j, 256 * j + 256)
            cols = slice(256 * i, 256 * i + 256)
            uh[rows, cols], ul[rows, cols] = split(t_ref[cols, rows].T)
    for source in range(8):
        start = (source % 2 * 4 + source // 2) * BLK
        at = slice(start, start + BLK)
        ph[at, :], pl_[at, :] = split(top_ref[source])

    for i in range(4):
        at, upto = slice(256 * i, 256 * i + 256), slice(0, 256 * i + 256)
        x = product((th[at, upto], tl[at, upto]), (ph[upto, :], pl_[upto, :]))
        fh[at, :], fl[at, :] = split(x)

    @pl.when(g == 0)
    def _():
        @pl.when(c == 0)
        def _():
            out_ref[...] = -first_ref[...]

        @pl.when(c == 1)
        def _():
            out_ref[:half, :] = jnp.zeros((half, half), jnp.float32)
            out_ref[half:, :] = -second_ref[half:, :]

        @pl.when(c >= 2)
        def _():
            out_ref[:half, :] = jnp.zeros((half, half), jnp.float32)
            left = split(first_ref[half:, :])
            out_ref[half:, :] = product(left, (fh[:half, :], fl[:half, :]))

    @pl.when(g > 0)
    def _():
        @pl.when(c == 0)
        def _():
            xh[...], xl[...] = -uh[:, :half], -ul[:, :half]

        @pl.when(c == 1)
        def _():
            xh[...], xl[...] = -uh[:, half:], -ul[:, half:]

        @pl.when(c >= 2)
        def _():
            for i in range(4):
                at, since = slice(256 * i, 256 * i + 256), slice(256 * i, LEAD)
                x = product((uh[at, since], ul[at, since]), (fh[since, :], fl[since, :]))
                xh[at, :], xl[at, :] = split(x)

        for sx in range(4):
            for sy in range(4):
                x, y = (px + 4 - sx) % 4, (py + 4 - sy) % 4
                where = x * 4 + y
                source = where // 2
                row = pl.multiple_of((where % 2) * half, half)
                column = pl.multiple_of(((source % 2) * 4 + source // 2) * BLK, BLK)
                tile = jnp.concatenate([pieces[sx][sy], pieces[4 + sy][sx]], axis=0).T
                to = (pl.ds(row, half), pl.ds(column, BLK))
                rh[to], rl[to] = split(tile)

        def update(at):
            out_ref[at, :] = product((rh[at, :], rl[at, :]), (xh[...], xl[...]))

        each(4, update)


def solve(place, inverse, first, second, top, pieces):
    def pair(rows, cols):
        return [pltpu.VMEM((rows, cols), jnp.bfloat16)] * 2

    return pl.pallas_call(
        solve_kernel,
        out_shape=jax.ShapeDtypeStruct((LEAD, PANEL), jnp.float32),
        in_specs=[TABLE] + [WHOLE] * 12,
        out_specs=WHOLE,
        scratch_shapes=pair(LEAD, LEAD) * 2 + pair(LEAD, PANEL) * 3 + pair(LEAD, LEAD),
        cost_estimate=work(10, 20),
        compiler_params=limit(36),
        name="solve",
    )(place, inverse, first, second, top, *pieces)


def schur_kernel(step_blocks, present_ref, absent_ref, rows_ref, high_ref, low_ref, out_ref, buf, zero, sem, zsem):
    step = pl.program_id(0)
    steps = pl.num_programs(0)
    slot = lax.rem(step, 2)

    def put(which, index, to):
        return pltpu.make_async_copy(
            buf.at[which, pl.ds(index * BLK, BLK)],
            out_ref.at[pl.ds(pl.multiple_of(to * BLK, BLK), BLK)],
            sem.at[which, index],
        )

    def clear(index, to):
        return pltpu.make_async_copy(
            zero, out_ref.at[pl.ds(pl.multiple_of(to * BLK, BLK), BLK)], zsem.at[index]
        )

    @pl.when(step == 0)
    def _():
        zero[...] = jnp.zeros_like(zero)

    for i in range(step_blocks):
        clear(i, absent_ref[step * step_blocks + i]).start()
    x = rows_ref[...]
    xh = x.astype(jnp.bfloat16)
    xl = (x - xh.astype(jnp.float32)).astype(jnp.bfloat16)
    wh = high_ref[...]
    total = jnp.dot(xh, wh, preferred_element_type=jnp.float32)
    total += jnp.dot(xh, low_ref[...], preferred_element_type=jnp.float32)
    total += jnp.dot(xl, wh, preferred_element_type=jnp.float32)

    @pl.when(step >= 2)
    def _():
        for i in range(step_blocks):
            put(slot, i, 0).wait()

    buf[slot] = total
    for i in range(step_blocks):
        put(slot, i, present_ref[step * step_blocks + i]).start()
    for i in range(step_blocks):
        clear(i, 0).wait()

    @pl.when(step == steps - 1)
    def _():
        for i in range(step_blocks):
            put(slot, i, 0).wait()
            put(1 - slot, i, 0).wait()


def schur_slab(present, absent, rows, high, low, step_blocks=4):
    width = high.shape[1]
    steps = SBLK // step_blocks
    return pl.pallas_call(
        functools.partial(schur_kernel, step_blocks),
        out_shape=jax.ShapeDtypeStruct((PBLK * BLK, width), jnp.float32),
        grid_spec=pltpu.PrefetchScalarGridSpec(
            num_scalar_prefetch=2,
            grid=(steps,),
            in_specs=[
                pl.BlockSpec((step_blocks * BLK, PIV), lambda i, p, a: (i, 0)),
                pl.BlockSpec((PIV, width), lambda i, p, a: (0, 0)),
                pl.BlockSpec((PIV, width), lambda i, p, a: (0, 0)),
            ],
            out_specs=pl.BlockSpec(memory_space=pltpu.HBM),
            scratch_shapes=[
                pltpu.VMEM((2, step_blocks * BLK, width), jnp.float32),
                pltpu.VMEM((BLK, width), jnp.float32),
                pltpu.SemaphoreType.DMA((2, step_blocks)),
                pltpu.SemaphoreType.DMA((step_blocks,)),
            ],
        ),
        cost_estimate=pl.CostEstimate(
            flops=6 * SBLK * BLK * PIV * width, bytes_accessed=36 << 20, transcendentals=0
        ),
        compiler_params=pltpu.CompilerParams(
            dimension_semantics=("arbitrary",), vmem_limit_bytes=58 << 20
        ),
        name="schur",
    )(present, absent, rows, high, low)


def swap_core(x):
    return lax.ppermute(x, "grp", [(i, i ^ 1) for i in range(8)])


def along_z(x, shift):
    return lax.ppermute(x, "grp", [(i, (i + 2 * shift) % 8) for i in range(8)])


def along_x(x, shift):
    return lax.ppermute(x, "col", [(i, (i + 4 * shift) % 16) for i in range(16)])


def along_y(x, shift):
    return lax.ppermute(x, "col", [(i, i // 4 * 4 + (i + shift) % 4) for i in range(16)])


def fetch(x, mover):
    return [x] + [mover(x, s) for s in (1, 2, 3)]


def plane_near(x):
    half = x.shape[0] // 2
    return jnp.stack(fetch(x[:half], along_y)), jnp.stack(fetch(x[half:], along_x))


def plane_far(near):
    return fetch(near[0], along_x) + fetch(near[1], along_y)


def pick(x, index, axis):
    return lax.dynamic_index_in_dim(x, index, axis, keepdims=False)


def after(value, *others):
    return lax.optimization_barrier((value, *others))[0]


def program(pivot_blocks, coupling, block_map, parent_matrix):
    g = lax.axis_index("grp")
    c = lax.axis_index("col")
    pz, core = g // 2, g % 2
    px, py = c // 4, c % 4
    at_top = g == 0
    place = jnp.stack([g, c, pz, core, px, py]).astype(jnp.int32)

    gathered = lax.all_gather(coupling[0], "col", axis=0, tiled=True)

    lead_own = []
    for s in range(8):
        row, column = PANEL * (s % 2), BLK * (s // 2)
        piece = parent_matrix[row : row + PANEL, column : column + BLK]
        lead_own.append(lax.ppermute(piece, ("grp", "col"), [(0, s), (1, 8 + s)]))

    mapping = pick(block_map, g, 0)
    spots = jnp.arange(PBLK, dtype=jnp.int32)
    matches = mapping[None, :] == spots[:, None]
    position = jnp.sum(jnp.where(matches, jnp.arange(SBLK, dtype=jnp.int32)[None, :], 0), axis=1)
    present = jnp.any(matches, axis=1)
    rank = jnp.sum((spots[None, :] < spots[:, None]) & ~present[None, :], axis=1)
    slots = jnp.arange(SBLK, dtype=jnp.int32)
    absent = jnp.sum(
        jnp.where((rank[None, :] == slots[:, None]) & ~present[None, :], spots[None, :], 0), axis=1
    ).astype(jnp.int32)
    n = jnp.arange(17, dtype=jnp.int32)
    side = jnp.where(n % 4 < 2, core, 1 - core)
    lead_spot = 4 * (c % 2) + 2 * side + n % 2
    top_side = jnp.where(n < 13, core, 1 - core)
    top_spot = 4 * top_side + (pz + n - 9) % 4
    spot = jnp.where(
        n < 4, lead_spot, jnp.where(n < 5, c // 2, jnp.where(n < 9, 4 * c + n - 5, top_spot))
    ).astype(jnp.int32)
    chosen = spot[:, None] == spots[None, :]
    where = jnp.sum(jnp.where(chosen, position[None, :], 0), axis=1)
    there = jnp.sum((chosen & present[None, :]).astype(jnp.int32), axis=1)

    pivot, mapping, where, there, absent, place, spot = lax.optimization_barrier(
        (pivot_blocks[0], mapping, where, there, absent, place, spot)
    )
    child_inv = child_factor(pivot)
    inv_high, inv_low, child_rows = child_rows_of(child_inv, coupling[0])
    own = lead_own[0]
    for more in lead_own[1:]:
        own = own + more
    gathered, child_rows, own = lax.optimization_barrier((gathered, child_rows, own))

    half_piece = jax.ShapeDtypeStruct((PANEL // 2, BLK), jnp.float32)
    lead_keep, lead_give = with_blocks(
        lead_part_kernel,
        5,
        [half_piece] * 2,
        (where[:5], there[:5], place),
        (inv_high, inv_low, own),
        gathered,
    )
    lead_got = swap_core(lead_give)
    wide = jax.ShapeDtypeStruct((PIV, PANEL), jnp.bfloat16)
    solved = with_blocks(
        solved_kernel, 4, [wide, wide], (where[5:9], there[5:9]), (inv_high, inv_low), gathered
    )

    half_top = jax.ShapeDtypeStruct((4, BLK, PANEL), jnp.float32)
    top_keep, top_give = with_blocks(
        top_kernel,
        8,
        [half_top] * 2,
        (where[9:], there[9:], spot[9:], place),
        (*solved, parent_matrix),
        gathered,
    )
    top_got = swap_core(top_give)
    lead_mine = lead_keep + lead_got
    others = [along_z(lead_mine, s) for s in (1, 2, 3)]
    top_mine = top_keep + top_got
    strips = [along_z(top_mine[s], s) for s in (1, 2, 3)]
    lead_mine = lead_mine + others[0] + others[1] + others[2]
    lead_other = swap_core(lead_mine)
    lead_near = (
        jnp.stack(fetch(lead_mine, along_y)),
        jnp.stack(fetch(lead_other, along_x)),
    )
    strip = top_mine[0] + strips[0] + strips[1] + strips[2]
    turn = [
        (gg * 16 + cc, (cc // 2) * 16 + 2 * gg + cc % 2) for gg in range(8) for cc in range(16)
    ]
    turned = lax.ppermute(strip, ("grp", "col"), turn)
    top_all = lax.all_gather(strip, "grp", axis=0)

    slab_all = schur_slab(mapping, absent, after(gathered, strip), *solved)
    update = lax.psum_scatter(slab_all, "grp", scatter_dimension=0, tiled=True)

    near_a, near_b, _, top_all = lax.optimization_barrier((*lead_near, slab_all, top_all))
    lead_far = plane_far((near_a, near_b))
    row_near = plane_near(turned)
    inv, low_first = lead_start(place, lead_far, 4)
    row_far = plane_far(row_near)
    inv, low_second = lead_next(inv, 4, 8)

    change = solve(place, inv, low_first, low_second, top_all, row_far)

    below = (g > 0) & (c >= 2)
    keep_first = below | (at_top & (c > 0))
    keep_second = c >= 2
    kept = jnp.where(jnp.arange(LEAD)[:, None] < PANEL, keep_first, keep_second)
    matrix = jnp.where(kept, after(parent_matrix, change) + update, 0.0) - change
    return (child_rows[None], matrix)


def solution(mesh):
    return jax.shard_map(
        program,
        mesh=mesh,
        in_specs=(P("grp", None, None), P("grp", "col", None), P(), P("grp", "col")),
        out_specs=(P("grp", "col", None), P("grp", "col")),
        check_vma=False,
    )
```
